128 devices in a mesh: seq: 4 (over z), head: 32 (over x, y, core).
Axes of the slice: x: 4, y: 4, z: 4, core: 2. Of those that a mesh axis runs over, the one named last changes fastest.
Arguments:
- inputs: bfloat16 [2048, 8192], P('seq'), may hold values from -6 to 6
- w_qkv: bfloat16 [3, 8192, 8192], P(None, None, 'head'), may hold values from -0.0625 to 0.0625
- w_out: bfloat16 [8192, 8192], P('head'), may hold values from -0.125 to 0.125
- turn_ids: int32 [4, 512], P('seq'), may hold values from 0 to 15, never falling along the last dimension, each value on 1 to 64 neighbouring positions
- picked: int32 [4, 64], P('seq'), may hold values from 0 to 511
- owners: int32 [256, 1], P('seq'), may hold values from 0 to 31; in each aligned block of 64 rows (0 to 63, 64 to 127, ...) at most 8 rows name the same one
- candidates: bfloat16 [8192, 8192], P(('seq', 'head')), may hold values from -0.25 to 0.25
Outputs:
- mixed: bfloat16 [2048, 8192], P('seq', 'head')
- scores: float32 [1024, 64], P(('seq', 'head'))
The draws below stay inside these ranges and needn't reach their ends.
Inputs may be any that keep to these rules, and one draw needn't show every extreme that they name: `turn_ids`: within each session turn numbers start at 0, never fall, and each turn has 1 to 64 tokens. `owners`: among the 64 picked rows of one session no owner is named more than 8 times.
All inputs are finite; a program needn't handle non-finite values.
Results may differ from the reference program's by a relative error of at most 0.008.
Values may be sent and summed in bfloat16 or wider, within the bound.
A program may use at most 128 MiB of HBM per device.

```python
import math
import jax
import jax.numpy as jnp
import numpy as np
from jax import lax

D = 8192
HDIM = 128
HEADS = 64
TOK_DEV = 512
TOKENS = 2048
TURNS = 16
TURN_MOST = 64
R_DEV = 64
SEL = 256
CAP = 8
NC = 64
CANDS = 8192
N_SEQ = 4
N_HEAD = 32


def plant(values, own_key, least, largest):
    extent = values.shape
    index_at = [jax.random.randint(jax.random.fold_in(own_key, axis), (), 0, extent[axis]) for axis in range(len(extent))]
    values = values.at[tuple(index_at)].set(least)
    longest = extent.index(max(extent))
    index_at[longest] = (index_at[longest] + 1) % extent[longest]
    return values.at[tuple(index_at)].set(largest)


def raised(result, own_key, source, target, parts, factor):
    owner, partner = [(jnp.arange(result.shape[axis_at]) // (result.shape[axis_at] // parts)).reshape([-1 if axis == axis_at else 1 for axis in range(result.ndim)]) for axis_at in (source, target)]
    chosen = jax.random.permutation(own_key, parts)[partner]
    strong = (owner == chosen) | (owner == (partner + parts // 2) % parts)
    return jnp.where(strong, factor * result, result)


def steps_of(stream_key, dims, cuts, least, top_value):
    def one(position, blocks):
        heights = jax.random.uniform(jax.random.fold_in(jax.random.fold_in(stream_key, 6), position), (blocks,), jnp.float32, least / len(cuts), top_value / len(cuts))
        return jnp.repeat(jnp.exp(heights), dims[position] // blocks).reshape((-1,) + (1,) * (len(dims) - position - 1))

    level = one(*cuts[0])
    for cut in cuts[1:]:
        level = level * one(*cut)
    return level


def length_profile(amount, total, reach, lean):
    weights = [(1 << 20) // math.isqrt(standing ** lean) + 1 for standing in range(2, amount + 1)]
    spare, counts = total - reach - (amount - 1), [1] * (amount - 1)
    while spare > 0:
        free = [i for i in range(amount - 1) if counts[i] < reach]
        pool, left = sum([weights[i] for i in free]), spare
        for i in free:
            addition = min(reach - counts[i], max(1, left * weights[i] // pool), spare)
            counts[i] = counts[i] + addition
            spare = spare - addition
    return np.array([reach] + counts)


def ragged_sizes(own_key, amount, total, most, slope):
    if amount == 2:
        one = jax.random.randint(own_key, (), max(1, total - most), min(most, total - 1) + 1)
        return jnp.stack([one, total - one])
    lengths = jnp.asarray(length_profile(amount, total, most, slope), jnp.int32)
    pairs = (amount - 1) // 2
    source_of, receiver = lengths[1:1 + 2 * pairs:2], lengths[2:2 + 2 * pairs:2]
    room = jnp.minimum(source_of - 1, most - receiver)
    passed = jax.random.randint(jax.random.fold_in(own_key, 1), (pairs,), 0, 1 << 20) % (room + 1)
    lengths = lengths.at[1:1 + 2 * pairs:2].set(source_of - passed).at[2:2 + 2 * pairs:2].set(receiver + passed)
    return lengths[jax.random.permutation(jax.random.fold_in(own_key, 2), amount)]


def routed_block(key, own, number, rows, number_of, top, limit, lean):
    sequence = jax.random.permutation(key, number_of)
    crowded, ordinary = portions_of(number_of, rows * top, limit, lean, True), portions_of(number_of, rows * top, limit, lean, False)
    places = jnp.arange(number_of)

    def named(sizes, turn):
        used = int((sizes > 0).sum())
        fixed = max(1, used // 4)
        shifted = fixed + (places - fixed + turn * (used - fixed)) % max(1, number_of - fixed)
        return jnp.zeros((number_of,), jnp.int32).at[sequence[jnp.where(places < fixed, places, shifted)]].set(jnp.asarray(sizes, jnp.int32))

    sizes = jnp.where(number % 4 == 0, named(crowded, number // 4), named(ordinary, number - number // 4 - 1))
    mixed = jax.random.permutation(jax.random.fold_in(own, 3), number_of)
    source_of, receiver = mixed[0:number_of // 2 * 2:2], mixed[1:number_of // 2 * 2:2]
    margin = jnp.minimum(sizes[source_of] - 1, limit - sizes[receiver]) // 2
    margin = jnp.where((source_of == sequence[0]) | (receiver == sequence[0]) | (sizes[receiver] == 0), 0, jnp.maximum(margin, 0))
    shifted = jax.random.randint(jax.random.fold_in(own, 4), (number_of // 2,), 0, 1 << 20) % (margin + 1)
    sizes = sizes.at[source_of].add(-shifted).at[receiver].add(shifted)
    labels = jnp.searchsorted(jnp.cumsum(sizes), jnp.arange(rows * top), side="right").astype(jnp.int32)
    listing = labels.reshape(top, rows).T
    listing = listing[jax.random.permutation(jax.random.fold_in(own, 1), rows)]
    turn = jax.random.randint(jax.random.fold_in(own, 2), (rows, 1), 0, top)
    return jnp.take_along_axis(listing, (jnp.arange(top)[None, :] + turn) % top, axis=1)


def portions_of(amount, total, reach, skew, full):
    weights = [(1 << 20) // math.isqrt(grade ** skew) + 1 for grade in range(1, amount + 1)]
    largest = reach if full else min(reach, max(-(-total // amount), total * weights[0] // sum(weights)))
    least = 1 if total - largest >= amount - 1 else 0
    holding, spare = [largest] + [least] * (amount - 1), total - largest - least * (amount - 1)
    while spare > 0:
        free = [i for i in range(1, amount) if holding[i] < largest] or [i for i in range(1, amount) if holding[i] < reach]
        pool, left = sum([weights[i] for i in free]), spare
        for i in free:
            addition = min(reach - holding[i], max(1, left * weights[i] // pool), spare)
            holding[i] = holding[i] + addition
            spare = spare - addition
    return np.array(holding)


def centred(own_key, extent, deviation, bound, cuts=(), held_as=jnp.bfloat16):
    result = jax.random.normal(own_key, extent, jnp.float32) * deviation
    if len(cuts) > 0:
        result = steps_of(own_key, extent, cuts, -0.22, 0.18) * result
    return jnp.clip(result, min=-bound, max=bound).astype(held_as)


def gaussian_with(own_key, dims, width, most, cuts, heavy, kind=jnp.bfloat16):
    result = width * jax.random.normal(own_key, dims, jnp.float32)
    if cuts:
        result = result * steps_of(own_key, dims, cuts, -0.22, 0.18)
    return jnp.clip(raised(result, jax.random.fold_in(own_key, 3), *heavy), -most, most).astype(kind)


def setup_inputs(seed: int = 0) -> dict:
    streams_of = jax.random.split(jax.random.key(seed), 8)
    inputs = centred(streams_of[0], (TOKENS, D), 1.0, 6.0, ((0, 4),))
    w_qkv = centred(streams_of[1], (3, D, HEADS * HDIM), D ** -0.5, 0.0625, ((2, 32),))
    w_out = gaussian_with(streams_of[2], (HEADS * HDIM, D), (HEADS * HDIM) ** -0.5, 0.125, ((0, 32),), (0, 1, 32, 2.75))
    turn_ids = jax.vmap(lambda own: jnp.searchsorted(jnp.cumsum(ragged_sizes(own, TURNS, TOK_DEV, TURN_MOST, 2)), jnp.arange(TOK_DEV), side="right"))(jax.random.split(streams_of[3], N_SEQ)).reshape((N_SEQ, TOK_DEV)).astype(jnp.int32)
    picked = plant(jax.random.randint(streams_of[4], (N_SEQ, R_DEV), 0, TOK_DEV), jax.random.fold_in(streams_of[4], 1), 0, TOK_DEV - 1).astype(jnp.int32)
    owners_keys = jax.random.split(jax.random.fold_in(streams_of[5], 1), SEL // R_DEV)
    owners_turns = jax.random.permutation(jax.random.fold_in(streams_of[5], 3), SEL // R_DEV)
    owners = jax.vmap(lambda own, number: routed_block(jax.random.fold_in(streams_of[5], 2), own, number, R_DEV, N_HEAD, 1, CAP, 2))(owners_keys, owners_turns).reshape((SEL, 1))
    candidates = centred(streams_of[6], (CANDS, D), (D // 16) ** -0.5, 0.25, ((0, 128),))
    return dict(inputs=inputs, w_qkv=w_qkv, w_out=w_out, turn_ids=turn_ids, picked=picked, owners=owners, candidates=candidates)


def session_block(operands):
    q_block, k_block, v_block, pre_state = operands
    raw_scores = jnp.einsum('thi,shi->hts', q_block.astype(jnp.float32), k_block.astype(jnp.float32))
    tok_pos = jnp.arange(q_block.shape[0], dtype=jnp.int32)
    causal = tok_pos[:, None] >= tok_pos[None, :]
    weights = jnp.where(causal[None, :, :], raw_scores, 0.0).astype(jnp.bfloat16)
    local_part = jnp.einsum('hts,shj->thj', weights.astype(jnp.float32), v_block.astype(jnp.float32))
    carried = jnp.einsum('thi,hij->thj', q_block.astype(jnp.float32), pre_state.astype(jnp.float32))
    summed = local_part + carried
    normed = summed * lax.rsqrt(lax.optimization_barrier(jnp.mean(summed * summed, axis=-1, keepdims=True)) + 1e-05)
    return normed.astype(jnp.bfloat16)

def reference(inputs, w_qkv, w_out, turn_ids, picked, owners, candidates):
    n_seq = turn_ids.shape[0]
    tok_dev = turn_ids.shape[1]
    head_count = w_qkv.shape[2] // HDIM
    projected = []
    for proj_index in range(3):
        projected.append(jnp.dot(inputs, w_qkv[proj_index], preferred_element_type=jnp.float32).astype(jnp.bfloat16))
    query = projected[0].reshape(n_seq, tok_dev, head_count, HDIM)
    keys = projected[1].reshape(n_seq, tok_dev, head_count, HDIM)
    values = projected[2].reshape(n_seq, tok_dev, head_count, HDIM)
    states = jnp.einsum('bthi,bthj->bhij', keys.astype(jnp.float32), values.astype(jnp.float32))
    zero_state = jnp.zeros((1,) + states.shape[1:], jnp.float32)
    prefix = jnp.cumsum(jnp.concatenate([zero_state, states[:-1]], axis=0), axis=0).astype(jnp.bfloat16)
    attended = lax.map(session_block, (query, keys, values, prefix))
    attended = attended.reshape(n_seq * tok_dev, head_count * HDIM)
    mixed_sum = inputs.astype(jnp.float32) + jnp.dot(attended, w_out, preferred_element_type=jnp.float32)
    mixed = mixed_sum.astype(jnp.bfloat16)
    mixed_rows = mixed.reshape(n_seq, tok_dev, mixed.shape[1])
    r_dev = picked.shape[1]
    n_head = candidates.shape[0] // (NC * n_seq)
    cap_rows = 4 * r_dev // n_head
    owner_rows = owners[:, 0].reshape(n_seq, r_dev)
    cand_rows = candidates.reshape(n_seq, n_head, NC, candidates.shape[1])
    tok_pos = jnp.arange(tok_dev, dtype=jnp.int32)
    row_pos = jnp.arange(r_dev, dtype=jnp.int32)
    head_pos = jnp.arange(n_head, dtype=jnp.int32)
    results = []
    for session in range(n_seq):
        turn_row = turn_ids[session]
        pick_row = picked[session]
        pick_hot = tok_pos[None, :] == pick_row[:, None]
        sel_turn = lax.optimization_barrier(jnp.sum(jnp.where(pick_hot, turn_row[None, :], 0), axis=1)).astype(jnp.int32)
        member = (turn_row[None, :] == sel_turn[:, None]) & (tok_pos[None, :] <= pick_row[:, None])
        row_count = lax.optimization_barrier(jnp.sum(member.astype(jnp.float32), axis=1))
        pooled = jnp.dot(member.astype(jnp.bfloat16), mixed_rows[session], preferred_element_type=jnp.float32)
        summary = (pooled / row_count[:, None]).astype(jnp.bfloat16)
        owner_row = owner_rows[session]
        own_hot = (owner_row[:, None] == head_pos[None, :]).astype(jnp.int32)
        before = (row_pos[:, None] > row_pos[None, :]).astype(jnp.int32)
        slot_rank = lax.optimization_barrier(jnp.sum(jnp.dot(before, own_hot) * own_hot, axis=1)).astype(jnp.int32)
        slot_index = owner_row * cap_rows + slot_rank
        buffer = jnp.zeros((n_head * cap_rows, summary.shape[1]), jnp.bfloat16).at[slot_index].set(summary)
        buffer = buffer.reshape(n_head, cap_rows, summary.shape[1])
        slot_scores = jnp.einsum('okd,ond->okn', buffer.astype(jnp.float32), cand_rows[session].astype(jnp.float32))
        results.append(slot_scores.reshape(n_head * cap_rows, NC))
    scores = jnp.concatenate(results, axis=0)
    return (mixed, scores)
```

```python
import functools

import jax
import jax.numpy as jnp
from jax import lax
from jax.experimental import pallas as pl
from jax.experimental.pallas import tpu as pltpu
from jax.sharding import PartitionSpec as P

HDIM = 128
SIDE = 4
KB = 1024
AHEAD = 4
NQ = 2
MESH = pl.DeviceIdType.MESH
BF = jnp.bfloat16
F32 = jnp.float32


def mm(a, b, dims=((1,), (0,))):
    return lax.dot_general(a, b, (dims, ((), ())), preferred_element_type=F32)


def kernel(
    x_hbm, wqkv_hbm, wout_hbm, turn_ref, picked_ref, owners_ref, cand_hbm,
    mixed_ref, scores_ref,
    xbuf, wbuf, acc, qkv, st, st_in, pre, a2, w2, c, r1, s1, r2, xcols, outb, inb, cand,
    xsem, wsem, msem, w2l, w2s, w2r, sts, strr, a2s, a2r, s1s, s1r, s2s, s2r, aas, aar,
):
    tokens, col = xcols.shape
    nk = xbuf.shape[0]
    n_head = outb.shape[0]
    n_seq = st_in.shape[0] + 1
    half = tokens // 2
    piece = half // NQ
    hp = piece // 2
    z = lax.axis_index("seq")
    me = lax.axis_index("head")
    core = lax.rem(me, 2)
    cy = lax.rem(lax.div(me, 2), SIDE)
    cx = lax.div(me, 2 * SIDE)

    def at(px, py, pc):
        return (px * SIDE + py) * 2 + pc

    sib = at(cx, cy, 1 - core)

    def x_load(k):
        return pltpu.make_async_copy(
            x_hbm.at[:, pl.ds(pl.multiple_of(k * KB, KB), KB)], xbuf.at[k], xsem.at[k]
        )

    def w_load(n, k):
        return pltpu.make_async_copy(
            wqkv_hbm.at[n, pl.ds(pl.multiple_of(k * KB, KB), KB), :], wbuf.at[n, k], wsem.at[n, k]
        )

    def remote(src, dst, ssem, rsem, to):
        return pltpu.make_async_remote_copy(
            src_ref=src, dst_ref=dst, send_sem=ssem, recv_sem=rsem, device_id=to, device_id_type=MESH
        )

    for k in range(AHEAD):
        x_load(k).start()
        w_load(1, k).start()
        w_load(2, k).start()

    barrier = pltpu.get_barrier_semaphore()

    def greet(i, carry):
        pl.semaphore_signal(
            barrier, inc=1, device_id={"head": lax.rem(me + i, n_head)}, device_id_type=MESH
        )
        return carry

    lax.fori_loop(1, n_head, greet, 0)
    for d in range(1, n_seq):
        pl.semaphore_signal(
            barrier, inc=1, device_id={"seq": lax.rem(z + d, n_seq)}, device_id_type=MESH
        )

    acc[...] = jnp.zeros_like(acc)

    def kv_step(k, carry):
        x_load(k).wait()
        w_load(1, k).wait()
        w_load(2, k).wait()

        @pl.when(k + AHEAD < nk)
        def _():
            x_load(k + AHEAD).start()
            w_load(1, k + AHEAD).start()
            w_load(2, k + AHEAD).start()

        @pl.when(k + AHEAD >= nk)
        def _():
            w_load(0, k + AHEAD - nk).start()

        acc[1] += mm(xbuf[k], wbuf[1, k])
        acc[2] += mm(xbuf[k], wbuf[2, k])
        return carry

    lax.fori_loop(0, nk, kv_step, 0)
    qkv[1] = acc[1].astype(BF)
    qkv[2] = acc[2].astype(BF)

    pl.semaphore_wait(barrier, n_head - 1 + n_seq - 1)

    for h in range(2):
        hs = slice(h * HDIM, (h + 1) * HDIM)
        st[h] = mm(qkv[1, :, hs], qkv[2, :, hs], ((0,), (0,))).astype(BF)
    state_copies = [
        remote(st, st_in.at[d - 1], sts.at[d - 1], strr.at[d - 1], {"seq": lax.rem(z + d, n_seq)})
        for d in range(1, n_seq)
    ]
    for cp in state_copies:
        cp.start()

    w2_local, w2_remote = [], []
    for j in range(SIDE * SIDE):
        jx, jy = j // SIDE, j % SIDE
        mine = pl.ds(pl.multiple_of((2 * j + core) * col, col), col)
        theirs = pl.ds(pl.multiple_of((2 * j + 1 - core) * col, col), col)
        w2_local.append(
            pltpu.make_async_copy(wout_hbm.at[:, mine], w2.at[jx, jy, core], w2l.at[j])
        )
        w2_remote.append(
            remote(wout_hbm.at[:, theirs], w2.at[jx, jy, core], w2s.at[j], w2r.at[j], {"head": sib})
        )
    for cp in w2_local + w2_remote:
        cp.start()
    x_cols = pltpu.make_async_copy(
        x_hbm.at[:, pl.ds(pl.multiple_of(me * col, col), col)], xcols, msem.at[0]
    )
    x_cols.start()
    cand_load = pltpu.make_async_copy(cand_hbm, cand, msem.at[1])
    cand_load.start()

    def q_step(k, carry):
        w_load(0, k).wait()

        @pl.when(k + AHEAD < nk)
        def _():
            w_load(0, k + AHEAD).start()

        acc[0] += mm(xbuf[k], wbuf[0, k])
        return carry

    lax.fori_loop(0, nk, q_step, 0)
    qkv[0] = acc[0].astype(BF)

    for b in range(2):
        rows = slice(b * half, (b + 1) * half)
        seen = (b + 1) * half
        ok = (
            lax.broadcasted_iota(jnp.int32, (half, seen), 0) + b * half
            >= lax.broadcasted_iota(jnp.int32, (half, seen), 1)
        )
        for h in range(2):
            hs = slice(h * HDIM, (h + 1) * HDIM)
            sc = mm(qkv[0, rows, hs], qkv[1, :seen, hs], ((1,), (1,)))
            sc = jnp.where(ok, sc, 0.0).astype(BF)
            pre[rows, hs] = mm(sc, qkv[2, :seen, hs])

    for cp in state_copies:
        cp.wait_recv()
    prefix = []
    for h in range(2):
        total = jnp.zeros((HDIM, HDIM), F32)
        for d in range(1, n_seq):
            total = total + jnp.where(z >= d, st_in[d - 1, h].astype(F32), 0.0)
        prefix.append(total.astype(BF))
    a2_copies = []
    for b in range(2):
        rows = slice(b * half, (b + 1) * half)
        for h in range(2):
            hs = slice(h * HDIM, (h + 1) * HDIM)
            summed = pre[rows, hs] + mm(qkv[0, rows, hs], prefix[h])
            normed = summed * lax.rsqrt(jnp.mean(summed * summed, axis=-1, keepdims=True) + 1e-05)
            a2[core, rows, hs] = normed.astype(BF)
        cp = remote(a2.at[core, rows], a2.at[core, rows], a2s.at[b], a2r.at[b], {"head": sib})
        cp.start()
        a2_copies.append(cp)
    for cp in w2_local:
        cp.wait()
    for cp in w2_remote:
        cp.wait_recv()

    spot = (cx, cy)

    def turn(p, by):
        return lax.rem(spot[p] + by + SIDE, SIDE)

    def neighbour(p, by):
        to = turn(p, by)
        return {"head": at(to, cy, core) if p == 0 else at(cx, to, core)}

    def multiply(p, by):
        i = turn(p, by)
        rows = slice(p * half, (p + 1) * half)
        for j in range(SIDE):
            jx, jy = (i, j) if p == 0 else (j, i)
            c[jx, jy, rows, :] = (
                mm(a2[0, rows], w2[jx, jy, 0]) + mm(a2[1, rows], w2[jx, jy, 1])
            ).astype(BF)

    pieces = [(p, n) for n in range(NQ) for p in range(2)]
    index = {u: i for i, u in enumerate(pieces)}
    sends = []

    def part(u, which):
        p, n = u
        start = p * half + n * piece + which * hp
        return slice(start, start + hp)

    def blocks(u, by, which):
        i = turn(u[0], by)
        rows = part(u, which)
        return c.at[i, :, rows, :] if u[0] == 0 else c.at[:, i, rows, :]

    def send1(u, kind, src):
        i = index[u]
        cp = remote(
            src, r1.at[i, kind], s1s.at[i, kind], s1r.at[i, kind], neighbour(u[0], (1, -1)[kind % 2])
        )
        cp.start()
        sends.append(cp)

    def got1(u, kind):
        i = index[u]
        remote(
            r1.at[i, kind], r1.at[i, kind], s1s.at[i, kind], s1r.at[i, kind], neighbour(u[0], 1)
        ).wait_recv()

    def send2(u, kind, src):
        i = index[u]
        cp = remote(
            src, r2.at[i, kind], s2s.at[i, kind], s2r.at[i, kind], neighbour(1 - u[0], (1, -1)[kind % 2])
        )
        cp.start()
        sends.append(cp)

    def got2(u, kind):
        i = index[u]
        remote(
            r2.at[i, kind], r2.at[i, kind], s2s.at[i, kind], s2r.at[i, kind], neighbour(1 - u[0], 1)
        ).wait_recv()

    def forward1(u):
        i = index[u]
        for kind, by, which in ((0, 1, 0), (1, -1, 1)):
            got1(u, kind)
            r1[i, kind] = (
                r1[i, kind].astype(F32) + blocks(u, by, which)[...].astype(F32)
            ).astype(BF)
            send1(u, kind + 4, r1.at[i, kind])

    def finish1(u):
        i = index[u]
        for kind in (2, 3, 4, 5):
            got1(u, kind)
        for which, one, two in ((0, 4, 3), (1, 5, 2)):
            s1[i, :, which * hp : (which + 1) * hp, :] = (
                blocks(u, 0, which)[...].astype(F32) + r1[i, one].astype(F32) + r1[i, two].astype(F32)
            ).astype(BF)
        rows = (slice(0, hp), slice(hp, 2 * hp))
        q = 1 - u[0]
        send2(u, 0, s1.at[i, turn(q, 2), rows[0]])
        send2(u, 1, s1.at[i, turn(q, 2), rows[1]])
        send2(u, 2, s1.at[i, turn(q, 1), rows[1]])
        send2(u, 3, s1.at[i, turn(q, -1), rows[0]])

    def forward2(u):
        i = index[u]
        q = 1 - u[0]
        for kind, by, rows in ((0, 1, slice(0, hp)), (1, -1, slice(hp, 2 * hp))):
            got2(u, kind)
            r2[i, kind] = (
                r2[i, kind].astype(F32) + s1[i, turn(q, by), rows].astype(F32)
            ).astype(BF)
            send2(u, kind + 4, r2.at[i, kind])

    def finish2(u):
        i = index[u]
        for kind in (2, 3, 4, 5):
            got2(u, kind)
        q = 1 - u[0]
        for which, one, two in ((0, 4, 3), (1, 5, 2)):
            rows = part(u, which)
            branch = (
                s1[i, turn(q, 0), which * hp : (which + 1) * hp].astype(F32)
                + r2[i, one].astype(F32)
                + r2[i, two].astype(F32)
            )
            mixed_ref[rows, :] = (xcols[rows, :].astype(F32) + branch).astype(BF)

    for p in range(2):
        a2_copies[p].wait_recv()
        multiply(p, 2)
        send1((p, 0), 0, blocks((p, 0), 2, 0))
        send1((p, 0), 1, blocks((p, 0), 2, 1))
    for p in range(2):
        multiply(p, 1)
        multiply(p, -1)
        send1((p, 0), 2, blocks((p, 0), 1, 1))
        send1((p, 0), 3, blocks((p, 0), -1, 0))
        for n in range(1, NQ):
            send1((p, n), 0, blocks((p, n), 2, 0))
            send1((p, n), 1, blocks((p, n), 2, 1))
    for p in range(2):
        multiply(p, 0)
    x_cols.wait()
    for n in range(NQ):
        for p in range(2):
            forward1((p, n))
            if n > 0:
                send1((p, n), 2, blocks((p, n), 1, 1))
                send1((p, n), 3, blocks((p, n), -1, 0))
        if n > 0:
            for p in range(2):
                finish1((p, n - 1))
            if n > 1:
                for p in range(2):
                    forward2((p, n - 2))
    if NQ > 1:
        for p in range(2):
            forward2((p, NQ - 2))
    for p in range(2):
        finish1((p, NQ - 1))
    for n in range(NQ - 1):
        for p in range(2):
            finish2((p, n))

    r_dev = owners_ref.shape[0]
    eye = lax.broadcasted_iota(jnp.int32, (r_dev, r_dev), 0)
    eye_col = lax.broadcasted_iota(jnp.int32, (r_dev, r_dev), 1)
    same_place = eye == eye_col
    pick = jnp.sum(
        jnp.where(same_place, jnp.broadcast_to(picked_ref[...], (r_dev, r_dev)), 0), axis=1, keepdims=True
    )
    turns = jnp.broadcast_to(turn_ref[...], (r_dev, tokens))
    places = lax.broadcasted_iota(jnp.int32, (r_dev, tokens), 1)
    own_turn = jnp.sum(jnp.where(places == pick, turns, 0), axis=1, keepdims=True)
    member = jnp.where((turns == own_turn) & (places <= pick), 1.0, 0.0)
    count = jnp.sum(member, axis=1, keepdims=True)
    own_col = jnp.broadcast_to(owners_ref[...], (r_dev, r_dev))
    own_row = jnp.sum(jnp.where(same_place, own_col, 0), axis=0, keepdims=True)
    rank = jnp.sum(jnp.where((own_col == own_row) & (eye < eye_col), 1, 0), axis=0, keepdims=True)
    cap = outb.shape[1]
    slot = own_row * cap + rank
    dispatch = jnp.where(
        lax.broadcasted_iota(jnp.int32, (n_head * cap, r_dev), 0) == slot, 1.0, 0.0
    ).astype(BF)

    for p in range(2):
        forward2((p, NQ - 1))
    for p in range(2):
        finish2((p, NQ - 1))

    summary = (mm(member.astype(BF), mixed_ref[...]) / count).astype(BF)
    outb[...] = mm(dispatch, summary).astype(BF).reshape(n_head, cap, col)
    mine = pl.ds(pl.multiple_of(me * col, col), col)
    keep = pltpu.make_async_copy(outb.at[me], inb.at[:, mine], msem.at[2])
    keep.start()

    def hand(i):
        to = lax.rem(me + i, n_head)
        return remote(outb.at[to], inb.at[:, mine], aas.at[i - 1], aar.at[i - 1], {"head": to})

    def hand_out(i, carry):
        hand(i).start()
        return carry

    lax.fori_loop(1, n_head, hand_out, 0)
    cand_load.wait()
    keep.wait()

    def take_in(i, carry):
        hand(i).wait()
        return carry

    lax.fori_loop(1, n_head, take_in, 0)
    scores_ref[...] = mm(inb[...], cand[...], ((1,), (1,)))

    for cp in state_copies + w2_remote + a2_copies + sends:
        cp.wait_send()


def per_device(inputs, w_qkv, w_out, turn_ids, picked, owners, candidates):
    tokens, width = inputs.shape
    n_head = lax.axis_size("head")
    n_seq = lax.axis_size("seq")
    col = width // n_head
    here = w_qkv.shape[2]
    r_dev = picked.shape[1]
    cap = 4 * r_dev // n_head
    nk = width // KB
    units = 2 * NQ
    hp = tokens // (4 * NQ)
    dma = pltpu.SemaphoreType.DMA
    anywhere = pl.BlockSpec(memory_space=pl.ANY)
    vmem = pl.BlockSpec(memory_space=pltpu.VMEM)
    return pl.pallas_call(
        kernel,
        out_shape=(
            jax.ShapeDtypeStruct((tokens, col), BF),
            jax.ShapeDtypeStruct((cap, candidates.shape[0]), F32),
        ),
        in_specs=[anywhere, anywhere, anywhere, vmem, vmem, vmem, anywhere],
        out_specs=(vmem, vmem),
        scratch_shapes=[
            pltpu.VMEM((nk, tokens, KB), BF),
            pltpu.VMEM((3, nk, KB, here), BF),
            pltpu.VMEM((3, tokens, here), F32),
            pltpu.VMEM((3, tokens, here), BF),
            pltpu.VMEM((2, HDIM, HDIM), BF),
            pltpu.VMEM((n_seq - 1, 2, HDIM, HDIM), BF),
            pltpu.VMEM((tokens, here), F32),
            pltpu.VMEM((2, tokens, here), BF),
            pltpu.VMEM((SIDE, SIDE, 2, here, col), BF),
            pltpu.VMEM((SIDE, SIDE, tokens, col), BF),
            pltpu.VMEM((units, 6, SIDE, hp, col), BF),
            pltpu.VMEM((units, SIDE, 2 * hp, col), BF),
            pltpu.VMEM((units, 6, hp, col), BF),
            pltpu.VMEM((tokens, col), BF),
            pltpu.VMEM((n_head, cap, col), BF),
            pltpu.VMEM((cap, width), BF),
            pltpu.VMEM(candidates.shape, BF),
            dma((nk,)),
            dma((3, nk)),
            dma((3,)),
            dma((SIDE * SIDE,)),
            dma((SIDE * SIDE,)),
            dma((SIDE * SIDE,)),
            dma((n_seq - 1,)),
            dma((n_seq - 1,)),
            dma((2,)),
            dma((2,)),
            dma((units, 6)),
            dma((units, 6)),
            dma((units, 6)),
            dma((units, 6)),
            dma((n_head - 1,)),
            dma((n_head - 1,)),
        ],
        compiler_params=pltpu.CompilerParams(
            collective_id=0, has_side_effects=True, vmem_limit_bytes=58 << 20
        ),
    )(inputs, w_qkv, w_out, turn_ids, picked, owners, candidates)


def solution(mesh):
    return jax.shard_map(
        per_device,
        mesh=mesh,
        in_specs=(
            P("seq", None),
            P(None, None, "head"),
            P("head", None),
            P("seq", None),
            P("seq", None),
            P("seq", None),
            P(("seq", "head"), None),
        ),
        out_specs=(P("seq", "head"), P(("seq", "head"), None)),
        check_vma=False,
    )
```

```python
import functools

import jax
import jax.numpy as jnp
from jax import lax
from jax.experimental import pallas as pl
from jax.experimental.pallas import tpu as pltpu
from jax.sharding import PartitionSpec as P

HDIM = 128
SIDE = 4
KB = 1024
AHEAD = 4
MEET = 4
NQ = 2
MESH = pl.DeviceIdType.MESH
BF = jnp.bfloat16
F32 = jnp.float32


def mm(a, b, dims=((1,), (0,))):
    return lax.dot_general(a, b, (dims, ((), ())), preferred_element_type=F32)


def kernel(
    x_hbm, wqkv_hbm, wout_hbm, turn_hbm, picked_hbm, owners_hbm, cand_hbm,
    mixed_ref, scores_ref,
    xbuf, wbuf, acc, qkv, st, st_in, pre, a2, w2, c, r1, s1, r2, xcols, outb, inb, cand, turn_ref, picked_ref, owners_ref,
    xsem, wsem, qsem, msem, w2l, w2s, w2r, sts, strr, a2s, a2r, s1s, s1r, s2s, s2r, aas, aar,
):
    tokens, col = xcols.shape
    nk = xbuf.shape[0]
    n_head = outb.shape[0]
    n_seq = st_in.shape[0] + 1
    block = tokens // NQ
    piece = block // 2
    hp = piece // 2
    z = lax.axis_index("seq")
    me = lax.axis_index("head")
    core = lax.rem(me, 2)
    cy = lax.rem(lax.div(me, 2), SIDE)
    cx = lax.div(me, 2 * SIDE)

    def at(px, py, pc):
        return (px * SIDE + py) * 2 + pc

    sib = at(cx, cy, 1 - core)

    def x_load(k):
        return pltpu.make_async_copy(
            x_hbm.at[:, pl.ds(pl.multiple_of(k * KB, KB), KB)], xbuf.at[k], xsem.at[k]
        )

    def kv_load(k):
        rows = pl.ds(pl.multiple_of(k * KB, KB), KB)
        return pltpu.make_async_copy(
            wqkv_hbm.at[pl.ds(1, 2), rows, :], wbuf.at[k, pl.ds(1, 2)], wsem.at[k]
        )

    def q_load(k):
        rows = pl.ds(pl.multiple_of(k * KB, KB), KB)
        return pltpu.make_async_copy(wqkv_hbm.at[0, rows, :], wbuf.at[k, 0], qsem.at[k])

    def remote(src, dst, ssem, rsem, to):
        return pltpu.make_async_remote_copy(
            src_ref=src, dst_ref=dst, send_sem=ssem, recv_sem=rsem, device_id=to, device_id_type=MESH
        )

    for k in range(AHEAD):
        kv_load(k).start()
        x_load(k).start()

    barrier = pltpu.get_barrier_semaphore()

    def greet(i, carry):
        pl.semaphore_signal(
            barrier, inc=1, device_id={"head": lax.rem(me + i, n_head)}, device_id_type=MESH
        )
        return carry

    lax.fori_loop(1, n_head, greet, 0)
    for d in range(1, n_seq):
        pl.semaphore_signal(
            barrier, inc=1, device_id={"seq": lax.rem(z + d, n_seq)}, device_id_type=MESH
        )

    acc[...] = jnp.zeros_like(acc)

    def kv_step(k, carry):
        x_load(k).wait()
        kv_load(k).wait()

        @pl.when(k + AHEAD < nk)
        def _():
            kv_load(k + AHEAD).start()
            x_load(k + AHEAD).start()

        @pl.when(k + AHEAD >= nk)
        def _():
            q_load(k + AHEAD - nk).start()

        acc[1] += mm(xbuf[k], wbuf[k, 1])
        acc[2] += mm(xbuf[k], wbuf[k, 2])
        return carry

    lax.fori_loop(0, MEET, kv_step, 0)

    pl.semaphore_wait(barrier, n_head - 1 + n_seq - 1)

    w2_local, w2_remote = [], []
    for j in range(SIDE * SIDE):
        jx, jy = j // SIDE, j % SIDE
        mine = pl.ds(pl.multiple_of((2 * j + core) * col, col), col)
        theirs = pl.ds(pl.multiple_of((2 * j + 1 - core) * col, col), col)
        w2_local.append(
            pltpu.make_async_copy(wout_hbm.at[:, mine], w2.at[jx, jy, core], w2l.at[j])
        )
        w2_remote.append(
            remote(wout_hbm.at[:, theirs], w2.at[jx, jy, core], w2s.at[j], w2r.at[j], {"head": sib})
        )
    for cp in w2_local + w2_remote:
        cp.start()

    lax.fori_loop(MEET, nk, kv_step, 0)
    qkv[1] = acc[1].astype(BF)
    qkv[2] = acc[2].astype(BF)

    for h in range(2):
        hs = slice(h * HDIM, (h + 1) * HDIM)
        st[h] = mm(qkv[1, :, hs], qkv[2, :, hs], ((0,), (0,))).astype(BF)
    state_copies = [
        remote(st, st_in.at[d - 1], sts.at[d - 1], strr.at[d - 1], {"seq": lax.rem(z + d, n_seq)})
        for d in range(1, n_seq)
    ]
    for cp in state_copies:
        cp.start()

    x_cols = pltpu.make_async_copy(
        x_hbm.at[:, pl.ds(pl.multiple_of(me * col, col), col)], xcols, msem.at[0]
    )
    x_cols.start()
    cand_load = pltpu.make_async_copy(cand_hbm, cand, msem.at[1])
    cand_load.start()
    small_loads = [
        pltpu.make_async_copy(src, dst, msem.at[3 + i])
        for i, (src, dst) in enumerate(
            ((turn_hbm, turn_ref), (picked_hbm, picked_ref), (owners_hbm, owners_ref))
        )
    ]
    for cp in small_loads:
        cp.start()

    def q_step(k, carry):
        q_load(k).wait()

        @pl.when(k + AHEAD < nk)
        def _():
            q_load(k + AHEAD).start()

        acc[0] += mm(xbuf[k], wbuf[k, 0])
        return carry

    lax.fori_loop(0, nk, q_step, 0)
    qkv[0] = acc[0].astype(BF)

    def local(b):
        rows = slice(b * block, (b + 1) * block)
        seen = (b + 1) * block
        ok = (
            lax.broadcasted_iota(jnp.int32, (block, seen), 0) + b * block
            >= lax.broadcasted_iota(jnp.int32, (block, seen), 1)
        )
        for h in range(2):
            hs = slice(h * HDIM, (h + 1) * HDIM)
            sc = mm(qkv[0, rows, hs], qkv[1, :seen, hs], ((1,), (1,)))
            sc = jnp.where(ok, sc, 0.0).astype(BF)
            pre[rows, hs] = mm(sc, qkv[2, :seen, hs])

    def attend(b, prefix):
        rows = slice(b * block, (b + 1) * block)
        for h in range(2):
            hs = slice(h * HDIM, (h + 1) * HDIM)
            summed = pre[rows, hs] + mm(qkv[0, rows, hs], prefix[h])
            normed = summed * lax.rsqrt(jnp.mean(summed * summed, axis=-1, keepdims=True) + 1e-05)
            a2[core, rows, hs] = normed.astype(BF)
        cp = remote(a2.at[core, rows], a2.at[core, rows], a2s.at[b], a2r.at[b], {"head": sib})
        cp.start()
        return cp

    local(0)
    for cp in state_copies:
        cp.wait_recv()
    prefix = []
    for h in range(2):
        total = jnp.zeros((HDIM, HDIM), F32)
        for d in range(1, n_seq):
            total = total + jnp.where(z >= d, st_in[d - 1, h].astype(F32), 0.0)
        prefix.append(total.astype(BF))
    a2_copies = [attend(0, prefix)]
    for b in range(1, NQ):
        local(b)
        a2_copies.append(attend(b, prefix))
    for cp in w2_local:
        cp.wait()
    for cp in w2_remote:
        cp.wait_recv()

    spot = (cx, cy)

    def turn(p, by):
        return lax.rem(spot[p] + by + SIDE, SIDE)

    def neighbour(p, by):
        to = turn(p, by)
        return {"head": at(to, cy, core) if p == 0 else at(cx, to, core)}

    def multiply(n, places):
        rows = slice(n * block, (n + 1) * block)
        for bx, by in places:
            jx, jy = turn(0, bx), turn(1, by)
            c[jx, jy, rows, :] = (
                mm(a2[0, rows], w2[jx, jy, 0]) + mm(a2[1, rows], w2[jx, jy, 1])
            ).astype(BF)

    pieces = [(p, n) for n in range(NQ) for p in range(2)]
    index = {u: i for i, u in enumerate(pieces)}
    sends = []

    def part(u, which):
        p, n = u
        start = n * block + p * piece + which * hp
        return slice(start, start + hp)

    def blocks(u, by, which):
        i = turn(u[0], by)
        rows = part(u, which)
        return c.at[i, :, rows, :] if u[0] == 0 else c.at[:, i, rows, :]

    def send1(u, kind, src):
        i = index[u]
        cp = remote(
            src, r1.at[i, kind], s1s.at[i, kind], s1r.at[i, kind], neighbour(u[0], (1, -1)[kind % 2])
        )
        cp.start()
        sends.append(cp)

    def got1(u, kind):
        i = index[u]
        remote(
            r1.at[i, kind], r1.at[i, kind], s1s.at[i, kind], s1r.at[i, kind], neighbour(u[0], 1)
        ).wait_recv()

    def send2(u, kind, src):
        i = index[u]
        cp = remote(
            src, r2.at[i, kind], s2s.at[i, kind], s2r.at[i, kind], neighbour(1 - u[0], (1, -1)[kind % 2])
        )
        cp.start()
        sends.append(cp)

    def got2(u, kind):
        i = index[u]
        remote(
            r2.at[i, kind], r2.at[i, kind], s2s.at[i, kind], s2r.at[i, kind], neighbour(1 - u[0], 1)
        ).wait_recv()

    def forward1(u):
        i = index[u]
        for kind, by, which in ((0, 1, 0), (1, -1, 1)):
            got1(u, kind)
            r1[i, kind] = (
                r1[i, kind].astype(F32) + blocks(u, by, which)[...].astype(F32)
            ).astype(BF)
            send1(u, kind + 4, r1.at[i, kind])

    def finish1(u):
        i = index[u]
        for kind in (2, 3, 4, 5):
            got1(u, kind)
        for which, one, two in ((0, 4, 3), (1, 5, 2)):
            s1[i, :, which * hp : (which + 1) * hp, :] = (
                blocks(u, 0, which)[...].astype(F32) + r1[i, one].astype(F32) + r1[i, two].astype(F32)
            ).astype(BF)
        rows = (slice(0, hp), slice(hp, 2 * hp))
        q = 1 - u[0]
        send2(u, 0, s1.at[i, turn(q, 2), rows[0]])
        send2(u, 1, s1.at[i, turn(q, 2), rows[1]])
        send2(u, 2, s1.at[i, turn(q, 1), rows[1]])
        send2(u, 3, s1.at[i, turn(q, -1), rows[0]])

    def forward2(u):
        i = index[u]
        q = 1 - u[0]
        for kind, by, rows in ((0, 1, slice(0, hp)), (1, -1, slice(hp, 2 * hp))):
            got2(u, kind)
            r2[i, kind] = (
                r2[i, kind].astype(F32) + s1[i, turn(q, by), rows].astype(F32)
            ).astype(BF)
            send2(u, kind + 4, r2.at[i, kind])

    def finish2(u):
        i = index[u]
        for kind in (2, 3, 4, 5):
            got2(u, kind)
        q = 1 - u[0]
        for which, one, two in ((0, 4, 3), (1, 5, 2)):
            rows = part(u, which)
            branch = (
                s1[i, turn(q, 0), which * hp : (which + 1) * hp].astype(F32)
                + r2[i, one].astype(F32)
                + r2[i, two].astype(F32)
            )
            mixed_ref[rows, :] = (xcols[rows, :].astype(F32) + branch).astype(BF)

    steps = (2, 1, -1, 0)
    first = [(2, b) for b in steps] + [(b, 2) for b in steps[1:]]
    second = [(a, b) for a in steps[1:] for b in steps[1:] if (a, b) != (0, 0)]

    for n in range(NQ):
        a2_copies[n].wait_recv()
        multiply(n, first)
        for p in range(2):
            send1((p, n), 0, blocks((p, n), 2, 0))
            send1((p, n), 1, blocks((p, n), 2, 1))
        if n > 0:
            for p in range(2):
                forward1((p, n - 1))
        multiply(n, second)
        for p in range(2):
            send1((p, n), 2, blocks((p, n), 1, 1))
            send1((p, n), 3, blocks((p, n), -1, 0))
        multiply(n, [(0, 0)])
    x_cols.wait()
    for p in range(2):
        forward1((p, NQ - 1))
    for n in range(NQ - 1):
        for p in range(2):
            finish1((p, n))
        for p in range(2):
            forward2((p, n))
    for p in range(2):
        finish1((p, NQ - 1))
    for n in range(NQ - 1):
        for p in range(2):
            finish2((p, n))

    for cp in small_loads:
        cp.wait()
    r_dev = owners_ref.shape[1]
    eye = lax.broadcasted_iota(jnp.int32, (r_dev, r_dev), 0)
    eye_col = lax.broadcasted_iota(jnp.int32, (r_dev, r_dev), 1)
    same_place = eye == eye_col
    pick = jnp.sum(
        jnp.where(same_place, jnp.broadcast_to(picked_ref[...], (r_dev, r_dev)), 0), axis=1, keepdims=True
    )
    turns = jnp.broadcast_to(turn_ref[...], (r_dev, tokens))
    places = lax.broadcasted_iota(jnp.int32, (r_dev, tokens), 1)
    own_turn = jnp.sum(jnp.where(places == pick, turns, 0), axis=1, keepdims=True)
    member = jnp.where((turns == own_turn) & (places <= pick), 1.0, 0.0)
    count = jnp.sum(member, axis=1, keepdims=True)
    own_row = owners_ref[...]
    own_col = jnp.sum(
        jnp.where(same_place, jnp.broadcast_to(own_row, (r_dev, r_dev)), 0), axis=1, keepdims=True
    )
    rank = jnp.sum(jnp.where((own_col == own_row) & (eye < eye_col), 1, 0), axis=0, keepdims=True)
    cap = outb.shape[1]
    slot = own_row * cap + rank
    dispatch = jnp.where(
        lax.broadcasted_iota(jnp.int32, (n_head * cap, r_dev), 0) == slot, 1.0, 0.0
    ).astype(BF)

    for p in range(2):
        forward2((p, NQ - 1))
    for p in range(2):
        finish2((p, NQ - 1))

    summary = (mm(member.astype(BF), mixed_ref[...]) / count).astype(BF)
    outb[...] = mm(dispatch, summary).astype(BF).reshape(n_head, cap, col)
    mine = pl.ds(pl.multiple_of(me * col, col), col)
    keep = pltpu.make_async_copy(outb.at[me], inb.at[:, mine], msem.at[2])
    keep.start()

    def hand(i):
        to = lax.rem(me + i, n_head)
        return remote(outb.at[to], inb.at[:, mine], aas.at[i - 1], aar.at[i - 1], {"head": to})

    def hand_out(i, carry):
        hand(i).start()
        return carry

    lax.fori_loop(1, n_head, hand_out, 0)
    cand_load.wait()
    keep.wait()

    def take_in(i, carry):
        hand(i).wait()
        return carry

    lax.fori_loop(1, n_head, take_in, 0)
    scores_ref[...] = mm(inb[...], cand[...], ((1,), (1,)))

    for cp in state_copies + w2_remote + a2_copies + sends:
        cp.wait_send()


def hand_over(mixed_in, scores_in, mixed_out, scores_out, sem):
    copies = [
        pltpu.make_async_copy(mixed_in, mixed_out, sem.at[0]),
        pltpu.make_async_copy(scores_in, scores_out, sem.at[1]),
    ]
    for cp in copies:
        cp.start()
    for cp in copies:
        cp.wait()


def per_device(inputs, w_qkv, w_out, turn_ids, picked, owners, candidates):
    tokens, width = inputs.shape
    n_head = lax.axis_size("head")
    n_seq = lax.axis_size("seq")
    col = width // n_head
    here = w_qkv.shape[2]
    r_dev = picked.shape[1]
    cap = 4 * r_dev // n_head
    nk = width // KB
    units = 2 * NQ
    hp = tokens // (4 * NQ)
    dma = pltpu.SemaphoreType.DMA
    hbm = pl.BlockSpec(memory_space=pltpu.HBM)
    vmem = pl.BlockSpec(memory_space=pltpu.VMEM)
    results = pl.pallas_call(
        kernel,
        out_shape=(
            jax.ShapeDtypeStruct((tokens, col), BF),
            jax.ShapeDtypeStruct((cap, candidates.shape[0]), F32),
        ),
        in_specs=[hbm] * 7,
        out_specs=(vmem, vmem),
        scratch_shapes=[
            pltpu.VMEM((nk, tokens, KB), BF),
            pltpu.VMEM((nk, 3, KB, here), BF),
            pltpu.VMEM((3, tokens, here), F32),
            pltpu.VMEM((3, tokens, here), BF),
            pltpu.VMEM((2, HDIM, HDIM), BF),
            pltpu.VMEM((n_seq - 1, 2, HDIM, HDIM), BF),
            pltpu.VMEM((tokens, here), F32),
            pltpu.VMEM((2, tokens, here), BF),
            pltpu.VMEM((SIDE, SIDE, 2, here, col), BF),
            pltpu.VMEM((SIDE, SIDE, tokens, col), BF),
            pltpu.VMEM((units, 6, SIDE, hp, col), BF),
            pltpu.VMEM((units, SIDE, 2 * hp, col), BF),
            pltpu.VMEM((units, 6, hp, col), BF),
            pltpu.VMEM((tokens, col), BF),
            pltpu.VMEM((n_head, cap, col), BF),
            pltpu.VMEM((cap, width), BF),
            pltpu.VMEM(candidates.shape, BF),
            pltpu.VMEM(turn_ids.shape, jnp.int32),
            pltpu.VMEM(picked.shape, jnp.int32),
            pltpu.VMEM((1, r_dev), jnp.int32),
            dma((nk,)),
            dma((nk,)),
            dma((nk,)),
            dma((6,)),
            dma((SIDE * SIDE,)),
            dma((SIDE * SIDE,)),
            dma((SIDE * SIDE,)),
            dma((n_seq - 1,)),
            dma((n_seq - 1,)),
            dma((NQ,)),
            dma((NQ,)),
            dma((units, 6)),
            dma((units, 6)),
            dma((units, 6)),
            dma((units, 6)),
            dma((n_head - 1,)),
            dma((n_head - 1,)),
        ],
        compiler_params=pltpu.CompilerParams(
            collective_id=0, has_side_effects=True, vmem_limit_bytes=53 << 20
        ),
    )(
        inputs,
        w_qkv,
        w_out,
        pltpu.with_memory_space_constraint(turn_ids, pltpu.HBM),
        pltpu.with_memory_space_constraint(picked, pltpu.HBM),
        pltpu.with_memory_space_constraint(owners.reshape(1, r_dev), pltpu.HBM),
        candidates,
    )
    return pl.pallas_call(
        hand_over,
        out_shape=tuple(jax.ShapeDtypeStruct(a.shape, a.dtype) for a in results),
        in_specs=[pl.BlockSpec(memory_space=pltpu.VMEM)] * 2,
        out_specs=(pl.BlockSpec(memory_space=pltpu.HBM),) * 2,
        scratch_shapes=[dma((2,))],
        compiler_params=pltpu.CompilerParams(vmem_limit_bytes=4 << 20),
    )(*results)


def solution(mesh):
    return jax.shard_map(
        per_device,
        mesh=mesh,
        in_specs=(
            P("seq", None),
            P(None, None, "head"),
            P("head", None),
            P("seq", None),
            P("seq", None),
            P("seq", None),
            P(("seq", "head"), None),
        ),
        out_specs=(P("seq", "head"), P(("seq", "head"), None)),
        check_vma=False,
    )
```

```python
import functools

import jax
import jax.numpy as jnp
from jax import lax
from jax.experimental import pallas as pl
from jax.experimental.pallas import tpu as pltpu
from jax.sharding import PartitionSpec as P

HDIM = 128
SIDE = 4
KB = 2048
AHEAD = 2
MEET = 2
NQ = 2
MESH = pl.DeviceIdType.MESH
BF = jnp.bfloat16
F32 = jnp.float32


def mm(a, b, dims=((1,), (0,))):
    return lax.dot_general(a, b, (dims, ((), ())), preferred_element_type=F32)


def kernel(
    x_hbm, wqkv_hbm, wout_hbm, turn_hbm, picked_hbm, owners_hbm, cand_hbm,
    mixed_ref, scores_ref,
    xbuf, wbuf, acc, qkv, st, st_in, carried, pre, a2, w2, c, r1, s1, r2, xcols, outb, inb, cand, turn_ref, picked_ref, owners_ref,
    xsem, wsem, qsem, msem, w2l, w2s, w2r, sts, strr, a2s, a2r, s1s, s1r, s2s, s2r, aas, aar,
):
    tokens, col = xcols.shape
    nk = xbuf.shape[0]
    n_head = outb.shape[0]
    n_seq = st_in.shape[0] + 1
    block = tokens // NQ
    piece = block // 2
    hp = piece // 2
    z = lax.axis_index("seq")
    me = lax.axis_index("head")
    core = lax.rem(me, 2)
    cy = lax.rem(lax.div(me, 2), SIDE)
    cx = lax.div(me, 2 * SIDE)

    def at(px, py, pc):
        return (px * SIDE + py) * 2 + pc

    sib = at(cx, cy, 1 - core)

    def x_load(k):
        return pltpu.make_async_copy(
            x_hbm.at[:, pl.ds(pl.multiple_of(k * KB, KB), KB)], xbuf.at[k], xsem.at[k]
        )

    def kv_load(k):
        rows = pl.ds(pl.multiple_of(k * KB, KB), KB)
        return pltpu.make_async_copy(
            wqkv_hbm.at[pl.ds(1, 2), rows, :], wbuf.at[k, pl.ds(1, 2)], wsem.at[k]
        )

    def q_load(k):
        rows = pl.ds(pl.multiple_of(k * KB, KB), KB)
        return pltpu.make_async_copy(wqkv_hbm.at[0, rows, :], wbuf.at[k, 0], qsem.at[k])

    def remote(src, dst, ssem, rsem, to):
        return pltpu.make_async_remote_copy(
            src_ref=src, dst_ref=dst, send_sem=ssem, recv_sem=rsem, device_id=to, device_id_type=MESH
        )

    for k in range(AHEAD):
        kv_load(k).start()
        x_load(k).start()

    barrier = pltpu.get_barrier_semaphore()

    def greet(i, carry):
        pl.semaphore_signal(
            barrier, inc=1, device_id={"head": lax.rem(me + i, n_head)}, device_id_type=MESH
        )
        return carry

    lax.fori_loop(1, n_head, greet, 0)
    for d in range(1, n_seq):
        pl.semaphore_signal(
            barrier, inc=1, device_id={"seq": lax.rem(z + d, n_seq)}, device_id_type=MESH
        )

    acc[...] = jnp.zeros_like(acc)

    def kv_step(k, carry):
        x_load(k).wait()
        kv_load(k).wait()

        @pl.when(k + AHEAD < nk)
        def _():
            kv_load(k + AHEAD).start()
            x_load(k + AHEAD).start()

        @pl.when(k + AHEAD >= nk)
        def _():
            q_load(k + AHEAD - nk).start()

        acc[1] += mm(xbuf[k], wbuf[k, 1])
        acc[2] += mm(xbuf[k], wbuf[k, 2])
        return carry

    lax.fori_loop(0, MEET, kv_step, 0)

    pl.semaphore_wait(barrier, n_head - 1 + n_seq - 1)

    w2_local, w2_remote = [], []
    for j in range(SIDE * SIDE):
        jx, jy = j // SIDE, j % SIDE
        mine = pl.ds(pl.multiple_of((2 * j + core) * col, col), col)
        theirs = pl.ds(pl.multiple_of((2 * j + 1 - core) * col, col), col)
        w2_local.append(
            pltpu.make_async_copy(wout_hbm.at[:, mine], w2.at[jx, jy, core], w2l.at[j])
        )
        w2_remote.append(
            remote(wout_hbm.at[:, theirs], w2.at[jx, jy, core], w2s.at[j], w2r.at[j], {"head": sib})
        )
    for cp in w2_local + w2_remote:
        cp.start()

    lax.fori_loop(MEET, nk, kv_step, 0)
    qkv[1] = acc[1].astype(BF)
    qkv[2] = acc[2].astype(BF)

    def state_copy(d, h):
        i = 2 * (d - 1) + h
        to = {"seq": lax.rem(z + d, n_seq)}
        return remote(st.at[h], st_in.at[d - 1, h], sts.at[i], strr.at[i], to)

    for h in range(2):
        hs = slice(h * HDIM, (h + 1) * HDIM)
        st[h] = mm(qkv[1, :, hs], qkv[2, :, hs], ((0,), (0,))).astype(BF)
        for d in range(1, n_seq):

            @pl.when(z + d < n_seq)
            def _():
                state_copy(d, h).start()

    x_cols = pltpu.make_async_copy(
        x_hbm.at[:, pl.ds(pl.multiple_of(me * col, col), col)], xcols, msem.at[0]
    )
    x_cols.start()
    cand_load = pltpu.make_async_copy(cand_hbm, cand, msem.at[1])
    cand_load.start()
    small_loads = [
        pltpu.make_async_copy(src, dst, msem.at[3 + i])
        for i, (src, dst) in enumerate(
            ((turn_hbm, turn_ref), (picked_hbm, picked_ref), (owners_hbm, owners_ref))
        )
    ]
    for cp in small_loads:
        cp.start()

    def q_step(k, carry):
        q_load(k).wait()

        @pl.when(k + AHEAD < nk)
        def _():
            q_load(k + AHEAD).start()

        acc[0] += mm(xbuf[k], wbuf[k, 0])
        return carry

    lax.fori_loop(0, nk, q_step, 0)
    qkv[0] = acc[0].astype(BF)

    def local(b):
        rows = slice(b * block, (b + 1) * block)
        seen = (b + 1) * block
        ok = (
            lax.broadcasted_iota(jnp.int32, (block, seen), 0) + b * block
            >= lax.broadcasted_iota(jnp.int32, (block, seen), 1)
        )
        for h in range(2):
            hs = slice(h * HDIM, (h + 1) * HDIM)
            sc = mm(qkv[0, rows, hs], qkv[1, :seen, hs], ((1,), (1,)))
            sc = jnp.where(ok, sc, 0.0).astype(BF)
            pre[rows, hs] = mm(sc, qkv[2, :seen, hs])

    def attend(b, prefix):
        rows = slice(b * block, (b + 1) * block)
        for h in range(2):
            hs = slice(h * HDIM, (h + 1) * HDIM)
            summed = pre[rows, hs] + mm(qkv[0, rows, hs], prefix[h])
            normed = summed * lax.rsqrt(jnp.mean(summed * summed, axis=-1, keepdims=True) + 1e-05)
            a2[core, rows, hs] = normed.astype(BF)
        cp = remote(a2.at[core, rows], a2.at[core, rows], a2s.at[b], a2r.at[b], {"head": sib})
        cp.start()
        return cp

    local(0)
    carried[...] = jnp.zeros_like(carried)
    for d in range(1, n_seq):

        @pl.when(z >= d)
        def _():
            for h in range(2):
                state_copy(d, h).wait_recv()
                carried[h] += st_in[d - 1, h].astype(F32)

    prefix = [carried[h].astype(BF) for h in range(2)]
    a2_copies = [attend(0, prefix)]
    for b in range(1, NQ):
        local(b)
        a2_copies.append(attend(b, prefix))
    for cp in w2_local:
        cp.wait()
    for cp in w2_remote:
        cp.wait_recv()

    spot = (cx, cy)

    def turn(p, by):
        return lax.rem(spot[p] + by + SIDE, SIDE)

    def neighbour(p, by):
        to = turn(p, by)
        return {"head": at(to, cy, core) if p == 0 else at(cx, to, core)}

    def multiply(n, places):
        rows = slice(n * block, (n + 1) * block)
        for bx, by in places:
            jx, jy = turn(0, bx), turn(1, by)
            c[jx, jy, rows, :] = (
                mm(a2[0, rows], w2[jx, jy, 0]) + mm(a2[1, rows], w2[jx, jy, 1])
            ).astype(BF)

    pieces = [(p, n) for n in range(NQ) for p in range(2)]
    index = {u: i for i, u in enumerate(pieces)}
    sends = []

    def part(u, which):
        p, n = u
        start = n * block + p * piece + which * hp
        return slice(start, start + hp)

    def blocks(u, by, which):
        i = turn(u[0], by)
        rows = part(u, which)
        return c.at[i, :, rows, :] if u[0] == 0 else c.at[:, i, rows, :]

    def send1(u, kind, src):
        i = index[u]
        cp = remote(
            src, r1.at[i, kind], s1s.at[i, kind], s1r.at[i, kind], neighbour(u[0], (1, -1)[kind % 2])
        )
        cp.start()
        sends.append(cp)

    def got1(u, kind):
        i = index[u]
        remote(
            r1.at[i, kind], r1.at[i, kind], s1s.at[i, kind], s1r.at[i, kind], neighbour(u[0], 1)
        ).wait_recv()

    def send2(u, kind, src):
        i = index[u]
        cp = remote(
            src, r2.at[i, kind], s2s.at[i, kind], s2r.at[i, kind], neighbour(1 - u[0], (1, -1)[kind % 2])
        )
        cp.start()
        sends.append(cp)

    def got2(u, kind):
        i = index[u]
        remote(
            r2.at[i, kind], r2.at[i, kind], s2s.at[i, kind], s2r.at[i, kind], neighbour(1 - u[0], 1)
        ).wait_recv()

    def forward1(u):
        i = index[u]
        for kind, by, which in ((0, 1, 0), (1, -1, 1)):
            got1(u, kind)
            r1[i, kind] = (
                r1[i, kind].astype(F32) + blocks(u, by, which)[...].astype(F32)
            ).astype(BF)
            send1(u, kind + 4, r1.at[i, kind])

    def finish1(u):
        i = index[u]
        for kind in (2, 3, 4, 5):
            got1(u, kind)
        for which, one, two in ((0, 4, 3), (1, 5, 2)):
            s1[i, :, which * hp : (which + 1) * hp, :] = (
                blocks(u, 0, which)[...].astype(F32) + r1[i, one].astype(F32) + r1[i, two].astype(F32)
            ).astype(BF)
        rows = (slice(0, hp), slice(hp, 2 * hp))
        q = 1 - u[0]
        send2(u, 0, s1.at[i, turn(q, 2), rows[0]])
        send2(u, 1, s1.at[i, turn(q, 2), rows[1]])
        send2(u, 2, s1.at[i, turn(q, 1), rows[1]])
        send2(u, 3, s1.at[i, turn(q, -1), rows[0]])

    def forward2(u):
        i = index[u]
        q = 1 - u[0]
        for kind, by, rows in ((0, 1, slice(0, hp)), (1, -1, slice(hp, 2 * hp))):
            got2(u, kind)
            r2[i, kind] = (
                r2[i, kind].astype(F32) + s1[i, turn(q, by), rows].astype(F32)
            ).astype(BF)
            send2(u, kind + 4, r2.at[i, kind])

    def finish2(u):
        i = index[u]
        for kind in (2, 3, 4, 5):
            got2(u, kind)
        q = 1 - u[0]
        for which, one, two in ((0, 4, 3), (1, 5, 2)):
            rows = part(u, which)
            branch = (
                s1[i, turn(q, 0), which * hp : (which + 1) * hp].astype(F32)
                + r2[i, one].astype(F32)
                + r2[i, two].astype(F32)
            )
            mixed_ref[rows, :] = (xcols[rows, :].astype(F32) + branch).astype(BF)

    steps = (2, 1, -1, 0)
    first = [(2, b) for b in steps] + [(b, 2) for b in steps[1:]]
    second = [(a, b) for a in steps[1:] for b in steps[1:] if (a, b) != (0, 0)]

    for n in range(NQ):
        a2_copies[n].wait_recv()
        multiply(n, first)
        for p in range(2):
            send1((p, n), 0, blocks((p, n), 2, 0))
            send1((p, n), 1, blocks((p, n), 2, 1))
        if n > 0:
            for p in range(2):
                forward1((p, n - 1))
        multiply(n, second)
        for p in range(2):
            send1((p, n), 2, blocks((p, n), 1, 1))
            send1((p, n), 3, blocks((p, n), -1, 0))
        multiply(n, [(0, 0)])
    x_cols.wait()
    for p in range(2):
        forward1((p, NQ - 1))
    for n in range(NQ - 1):
        for p in range(2):
            finish1((p, n))
        for p in range(2):
            forward2((p, n))
    for p in range(2):
        finish1((p, NQ - 1))
    for n in range(NQ - 1):
        for p in range(2):
            finish2((p, n))

    for cp in small_loads:
        cp.wait()
    r_dev = owners_ref.shape[1]
    eye = lax.broadcasted_iota(jnp.int32, (r_dev, r_dev), 0)
    eye_col = lax.broadcasted_iota(jnp.int32, (r_dev, r_dev), 1)
    same_place = eye == eye_col
    pick = jnp.sum(
        jnp.where(same_place, jnp.broadcast_to(picked_ref[...], (r_dev, r_dev)), 0), axis=1, keepdims=True
    )
    turns = jnp.broadcast_to(turn_ref[...], (r_dev, tokens))
    places = lax.broadcasted_iota(jnp.int32, (r_dev, tokens), 1)
    own_turn = jnp.sum(jnp.where(places == pick, turns, 0), axis=1, keepdims=True)
    member = jnp.where((turns == own_turn) & (places <= pick), 1.0, 0.0)
    count = jnp.sum(member, axis=1, keepdims=True)
    own_row = owners_ref[...]
    own_col = jnp.sum(
        jnp.where(same_place, jnp.broadcast_to(own_row, (r_dev, r_dev)), 0), axis=1, keepdims=True
    )
    rank = jnp.sum(jnp.where((own_col == own_row) & (eye < eye_col), 1, 0), axis=0, keepdims=True)
    cap = outb.shape[1]
    slot = own_row * cap + rank
    dispatch = jnp.where(
        lax.broadcasted_iota(jnp.int32, (n_head * cap, r_dev), 0) == slot, 1.0, 0.0
    ).astype(BF)

    for p in range(2):
        forward2((p, NQ - 1))
    for p in range(2):
        finish2((p, NQ - 1))

    summary = (mm(member.astype(BF), mixed_ref[...]) / count).astype(BF)
    outb[...] = mm(dispatch, summary).astype(BF).reshape(n_head, cap, col)
    mine = pl.ds(pl.multiple_of(me * col, col), col)
    keep = pltpu.make_async_copy(outb.at[me], inb.at[:, mine], msem.at[2])
    keep.start()

    def hand(i):
        to = lax.rem(me + i, n_head)
        return remote(outb.at[to], inb.at[:, mine], aas.at[i - 1], aar.at[i - 1], {"head": to})

    def hand_out(i, carry):
        hand(i).start()
        return carry

    lax.fori_loop(1, n_head, hand_out, 0)
    cand_load.wait()
    keep.wait()

    def take_in(i, carry):
        hand(i).wait()
        return carry

    lax.fori_loop(1, n_head, take_in, 0)
    scores_ref[...] = mm(inb[...], cand[...], ((1,), (1,)))

    for d in range(1, n_seq):

        @pl.when(z + d < n_seq)
        def _():
            for h in range(2):
                state_copy(d, h).wait_send()

    for cp in w2_remote + a2_copies + sends:
        cp.wait_send()


def hand_over(mixed_in, scores_in, mixed_out, scores_out, sem):
    copies = [
        pltpu.make_async_copy(mixed_in, mixed_out, sem.at[0]),
        pltpu.make_async_copy(scores_in, scores_out, sem.at[1]),
    ]
    for cp in copies:
        cp.start()
    for cp in copies:
        cp.wait()


def per_device(inputs, w_qkv, w_out, turn_ids, picked, owners, candidates):
    tokens, width = inputs.shape
    n_head = lax.axis_size("head")
    n_seq = lax.axis_size("seq")
    col = width // n_head
    here = w_qkv.shape[2]
    r_dev = picked.shape[1]
    cap = 4 * r_dev // n_head
    nk = width // KB
    units = 2 * NQ
    hp = tokens // (4 * NQ)
    dma = pltpu.SemaphoreType.DMA
    hbm = pl.BlockSpec(memory_space=pltpu.HBM)
    vmem = pl.BlockSpec(memory_space=pltpu.VMEM)
    results = pl.pallas_call(
        kernel,
        out_shape=(
            jax.ShapeDtypeStruct((tokens, col), BF),
            jax.ShapeDtypeStruct((cap, candidates.shape[0]), F32),
        ),
        in_specs=[hbm] * 7,
        out_specs=(vmem, vmem),
        scratch_shapes=[
            pltpu.VMEM((nk, tokens, KB), BF),
            pltpu.VMEM((nk, 3, KB, here), BF),
            pltpu.VMEM((3, tokens, here), F32),
            pltpu.VMEM((3, tokens, here), BF),
            pltpu.VMEM((2, HDIM, HDIM), BF),
            pltpu.VMEM((n_seq - 1, 2, HDIM, HDIM), BF),
            pltpu.VMEM((2, HDIM, HDIM), F32),
            pltpu.VMEM((tokens, here), F32),
            pltpu.VMEM((2, tokens, here), BF),
            pltpu.VMEM((SIDE, SIDE, 2, here, col), BF),
            pltpu.VMEM((SIDE, SIDE, tokens, col), BF),
            pltpu.VMEM((units, 6, SIDE, hp, col), BF),
            pltpu.VMEM((units, SIDE, 2 * hp, col), BF),
            pltpu.VMEM((units, 6, hp, col), BF),
            pltpu.VMEM((tokens, col), BF),
            pltpu.VMEM((n_head, cap, col), BF),
            pltpu.VMEM((cap, width), BF),
            pltpu.VMEM(candidates.shape, BF),
            pltpu.VMEM(turn_ids.shape, jnp.int32),
            pltpu.VMEM(picked.shape, jnp.int32),
            pltpu.VMEM((1, r_dev), jnp.int32),
            dma((nk,)),
            dma((nk,)),
            dma((nk,)),
            dma((6,)),
            dma((SIDE * SIDE,)),
            dma((SIDE * SIDE,)),
            dma((SIDE * SIDE,)),
            dma((2 * n_seq - 2,)),
            dma((2 * n_seq - 2,)),
            dma((NQ,)),
            dma((NQ,)),
            dma((units, 6)),
            dma((units, 6)),
            dma((units, 6)),
            dma((units, 6)),
            dma((n_head - 1,)),
            dma((n_head - 1,)),
        ],
        compiler_params=pltpu.CompilerParams(
            collective_id=0, has_side_effects=True, vmem_limit_bytes=53 << 20
        ),
    )(
        inputs,
        w_qkv,
        w_out,
        pltpu.with_memory_space_constraint(turn_ids, pltpu.HBM),
        pltpu.with_memory_space_constraint(picked, pltpu.HBM),
        pltpu.with_memory_space_constraint(owners.reshape(1, r_dev), pltpu.HBM),
        candidates,
    )
    return pl.pallas_call(
        hand_over,
        out_shape=tuple(jax.ShapeDtypeStruct(a.shape, a.dtype) for a in results),
        in_specs=[pl.BlockSpec(memory_space=pltpu.VMEM)] * 2,
        out_specs=(pl.BlockSpec(memory_space=pltpu.HBM),) * 2,
        scratch_shapes=[dma((2,))],
        compiler_params=pltpu.CompilerParams(vmem_limit_bytes=4 << 20),
    )(*results)


def solution(mesh):
    return jax.shard_map(
        per_device,
        mesh=mesh,
        in_specs=(
            P("seq", None),
            P(None, None, "head"),
            P("head", None),
            P("seq", None),
            P("seq", None),
            P("seq", None),
            P(("seq", "head"), None),
        ),
        out_specs=(P("seq", "head"), P(("seq", "head"), None)),
        check_vma=False,
    )
```

```python
import functools

import jax
import jax.numpy as jnp
from jax import lax
from jax.experimental import pallas as pl
from jax.experimental.pallas import tpu as pltpu
from jax.sharding import PartitionSpec as P

HDIM = 128
SIDE = 4
KB = 2048
AHEAD = 4
MEET = 3
NQ = 2
MESH = pl.DeviceIdType.MESH
BF = jnp.bfloat16
F32 = jnp.float32


def mm(a, b, dims=((1,), (0,))):
    return lax.dot_general(a, b, (dims, ((), ())), preferred_element_type=F32)


def kernel(
    x_hbm, wqkv_hbm, wout_hbm, turn_hbm, picked_hbm, owners_hbm, cand_hbm,
    mixed_ref, scores_ref,
    xbuf, wbuf, acc, qkv, st, st_in, carried, pre, a2, w2, c, r1, s1, r2, xcols, outb, inb, cand, turn_ref, picked_ref, owners_ref,
    xsem, wsem, qsem, msem, w2l, w2s, w2r, sts, strr, a2s, a2r, s1s, s1r, s2s, s2r, aas, aar,
):
    tokens, col = xcols.shape
    nk = xbuf.shape[0]
    n_head = outb.shape[0]
    n_seq = st_in.shape[0] + 1
    block = tokens // NQ
    piece = block // 2
    hp = piece // 2
    z = lax.axis_index("seq")
    me = lax.axis_index("head")
    core = lax.rem(me, 2)
    cy = lax.rem(lax.div(me, 2), SIDE)
    cx = lax.div(me, 2 * SIDE)

    def at(px, py, pc):
        return (px * SIDE + py) * 2 + pc

    sib = at(cx, cy, 1 - core)

    def x_load(k):
        return pltpu.make_async_copy(
            x_hbm.at[:, pl.ds(pl.multiple_of(k * KB, KB), KB)], xbuf.at[k], xsem.at[k]
        )

    def kv_load(k):
        rows = pl.ds(pl.multiple_of(k * KB, KB), KB)
        return pltpu.make_async_copy(
            wqkv_hbm.at[pl.ds(1, 2), rows, :], wbuf.at[k, pl.ds(1, 2)], wsem.at[k]
        )

    def q_load(k):
        rows = pl.ds(pl.multiple_of(k * KB, KB), KB)
        return pltpu.make_async_copy(wqkv_hbm.at[0, rows, :], wbuf.at[k, 0], qsem.at[k])

    def remote(src, dst, ssem, rsem, to):
        return pltpu.make_async_remote_copy(
            src_ref=src, dst_ref=dst, send_sem=ssem, recv_sem=rsem, device_id=to, device_id_type=MESH
        )

    for k in range(AHEAD):
        kv_load(k).start()
        x_load(k).start()

    barrier = pltpu.get_barrier_semaphore()

    def greet(i, carry):
        pl.semaphore_signal(
            barrier, inc=1, device_id={"head": lax.rem(me + i, n_head)}, device_id_type=MESH
        )
        return carry

    lax.fori_loop(1, n_head, greet, 0)
    for d in range(1, n_seq):
        pl.semaphore_signal(
            barrier, inc=1, device_id={"seq": lax.rem(z + d, n_seq)}, device_id_type=MESH
        )

    acc[...] = jnp.zeros_like(acc)

    def kv_step(k, carry):
        x_load(k).wait()
        kv_load(k).wait()

        @pl.when(k + AHEAD < nk)
        def _():
            kv_load(k + AHEAD).start()
            x_load(k + AHEAD).start()

        @pl.when(k + AHEAD >= nk)
        def _():
            q_load(k + AHEAD - nk).start()

        acc[1] += mm(xbuf[k], wbuf[k, 1])
        acc[2] += mm(xbuf[k], wbuf[k, 2])
        return carry

    lax.fori_loop(0, MEET, kv_step, 0)

    pl.semaphore_wait(barrier, n_head - 1 + n_seq - 1)

    w2_local, w2_remote = [], []
    for j in range(SIDE * SIDE):
        jx, jy = j // SIDE, j % SIDE
        mine = pl.ds(pl.multiple_of((2 * j + core) * col, col), col)
        theirs = pl.ds(pl.multiple_of((2 * j + 1 - core) * col, col), col)
        w2_local.append(
            pltpu.make_async_copy(wout_hbm.at[:, mine], w2.at[jx, jy, core], w2l.at[j])
        )
        w2_remote.append(
            remote(wout_hbm.at[:, theirs], w2.at[jx, jy, core], w2s.at[j], w2r.at[j], {"head": sib})
        )
    for cp in w2_local + w2_remote:
        cp.start()

    lax.fori_loop(MEET, nk, kv_step, 0)
    qkv[1] = acc[1].astype(BF)
    qkv[2] = acc[2].astype(BF)

    def state_copy(d, h):
        i = 2 * (d - 1) + h
        to = {"seq": lax.rem(z + d, n_seq)}
        return remote(st.at[h], st_in.at[d - 1, h], sts.at[i], strr.at[i], to)

    for h in range(2):
        hs = slice(h * HDIM, (h + 1) * HDIM)
        st[h] = mm(qkv[1, :, hs], qkv[2, :, hs], ((0,), (0,))).astype(BF)
        for d in range(1, n_seq):

            @pl.when(z + d < n_seq)
            def _():
                state_copy(d, h).start()

    x_cols = pltpu.make_async_copy(
        x_hbm.at[:, pl.ds(pl.multiple_of(me * col, col), col)], xcols, msem.at[0]
    )
    x_cols.start()
    cand_load = pltpu.make_async_copy(cand_hbm, cand, msem.at[1])
    cand_load.start()
    small_loads = [
        pltpu.make_async_copy(src, dst, msem.at[3 + i])
        for i, (src, dst) in enumerate(
            ((turn_hbm, turn_ref), (picked_hbm, picked_ref), (owners_hbm, owners_ref))
        )
    ]
    for cp in small_loads:
        cp.start()

    def q_step(k, carry):
        q_load(k).wait()

        @pl.when(k + AHEAD < nk)
        def _():
            q_load(k + AHEAD).start()

        acc[0] += mm(xbuf[k], wbuf[k, 0])
        return carry

    lax.fori_loop(0, nk, q_step, 0)
    qkv[0] = acc[0].astype(BF)

    def local(b):
        rows = slice(b * block, (b + 1) * block)
        seen = (b + 1) * block
        ok = (
            lax.broadcasted_iota(jnp.int32, (block, seen), 0) + b * block
            >= lax.broadcasted_iota(jnp.int32, (block, seen), 1)
        )
        for h in range(2):
            hs = slice(h * HDIM, (h + 1) * HDIM)
            sc = mm(qkv[0, rows, hs], qkv[1, :seen, hs], ((1,), (1,)))
            sc = jnp.where(ok, sc, 0.0).astype(BF)
            pre[rows, hs] = mm(sc, qkv[2, :seen, hs])

    def attend(b, prefix):
        rows = slice(b * block, (b + 1) * block)
        for h in range(2):
            hs = slice(h * HDIM, (h + 1) * HDIM)
            summed = pre[rows, hs] + mm(qkv[0, rows, hs], prefix[h])
            normed = summed * lax.rsqrt(jnp.mean(summed * summed, axis=-1, keepdims=True) + 1e-05)
            a2[core, rows, hs] = normed.astype(BF)
        cp = remote(a2.at[core, rows], a2.at[core, rows], a2s.at[b], a2r.at[b], {"head": sib})
        cp.start()
        return cp

    local(0)
    carried[...] = jnp.zeros_like(carried)
    for d in range(1, n_seq):

        @pl.when(z >= d)
        def _():
            for h in range(2):
                state_copy(d, h).wait_recv()
                carried[h] += st_in[d - 1, h].astype(F32)

    prefix = [carried[h].astype(BF) for h in range(2)]
    a2_copies = [attend(0, prefix)]
    for b in range(1, NQ):
        local(b)
        a2_copies.append(attend(b, prefix))
    for cp in w2_local:
        cp.wait()
    for cp in w2_remote:
        cp.wait_recv()

    spot = (cx, cy)

    def turn(p, by):
        return lax.rem(spot[p] + by + SIDE, SIDE)

    def neighbour(p, by):
        to = turn(p, by)
        return {"head": at(to, cy, core) if p == 0 else at(cx, to, core)}

    def multiply(n, places):
        rows = slice(n * block, (n + 1) * block)
        for bx, by in places:
            jx, jy = turn(0, bx), turn(1, by)
            c[jx, jy, rows, :] = (
                mm(a2[0, rows], w2[jx, jy, 0]) + mm(a2[1, rows], w2[jx, jy, 1])
            ).astype(BF)

    pieces = [(p, n) for n in range(NQ) for p in range(2)]
    index = {u: i for i, u in enumerate(pieces)}
    sends = []

    def part(u, which):
        p, n = u
        start = n * block + p * piece + which * hp
        return slice(start, start + hp)

    def blocks(u, by, which):
        i = turn(u[0], by)
        rows = part(u, which)
        return c.at[i, :, rows, :] if u[0] == 0 else c.at[:, i, rows, :]

    def send1(u, kind, src):
        i = index[u]
        cp = remote(
            src, r1.at[i, kind], s1s.at[i, kind], s1r.at[i, kind], neighbour(u[0], (1, -1)[kind % 2])
        )
        cp.start()
        sends.append(cp)

    def got1(u, kind):
        i = index[u]
        remote(
            r1.at[i, kind], r1.at[i, kind], s1s.at[i, kind], s1r.at[i, kind], neighbour(u[0], 1)
        ).wait_recv()

    def send2(u, kind, src):
        i = index[u]
        cp = remote(
            src, r2.at[i, kind], s2s.at[i, kind], s2r.at[i, kind], neighbour(1 - u[0], (1, -1)[kind % 2])
        )
        cp.start()
        sends.append(cp)

    def got2(u, kind):
        i = index[u]
        remote(
            r2.at[i, kind], r2.at[i, kind], s2s.at[i, kind], s2r.at[i, kind], neighbour(1 - u[0], 1)
        ).wait_recv()

    def forward1(u):
        i = index[u]
        for kind, by, which in ((0, 1, 0), (1, -1, 1)):
            got1(u, kind)
            r1[i, kind] = (
                r1[i, kind].astype(F32) + blocks(u, by, which)[...].astype(F32)
            ).astype(BF)
            send1(u, kind + 4, r1.at[i, kind])

    def finish1(u):
        i = index[u]
        for kind in (2, 3, 4, 5):
            got1(u, kind)
        for which, one, two in ((0, 4, 3), (1, 5, 2)):
            s1[i, :, which * hp : (which + 1) * hp, :] = (
                blocks(u, 0, which)[...].astype(F32) + r1[i, one].astype(F32) + r1[i, two].astype(F32)
            ).astype(BF)
        rows = (slice(0, hp), slice(hp, 2 * hp))
        q = 1 - u[0]
        send2(u, 0, s1.at[i, turn(q, 2), rows[0]])
        send2(u, 1, s1.at[i, turn(q, 2), rows[1]])
        send2(u, 2, s1.at[i, turn(q, 1), rows[1]])
        send2(u, 3, s1.at[i, turn(q, -1), rows[0]])

    def forward2(u):
        i = index[u]
        q = 1 - u[0]
        for kind, by, rows in ((0, 1, slice(0, hp)), (1, -1, slice(hp, 2 * hp))):
            got2(u, kind)
            r2[i, kind] = (
                r2[i, kind].astype(F32) + s1[i, turn(q, by), rows].astype(F32)
            ).astype(BF)
            send2(u, kind + 4, r2.at[i, kind])

    def finish2(u):
        i = index[u]
        for kind in (2, 3, 4, 5):
            got2(u, kind)
        q = 1 - u[0]
        for which, one, two in ((0, 4, 3), (1, 5, 2)):
            rows = part(u, which)
            branch = (
                s1[i, turn(q, 0), which * hp : (which + 1) * hp].astype(F32)
                + r2[i, one].astype(F32)
                + r2[i, two].astype(F32)
            )
            mixed_ref[rows, :] = (xcols[rows, :].astype(F32) + branch).astype(BF)

    steps = (2, 1, -1, 0)
    first = [(2, b) for b in steps] + [(b, 2) for b in steps[1:]]
    second = [(a, b) for a in steps[1:] for b in steps[1:] if (a, b) != (0, 0)]

    for n in range(NQ):
        a2_copies[n].wait_recv()
        multiply(n, first)
        for p in range(2):
            send1((p, n), 0, blocks((p, n), 2, 0))
            send1((p, n), 1, blocks((p, n), 2, 1))
        if n > 0:
            for p in range(2):
                forward1((p, n - 1))
        multiply(n, second)
        for p in range(2):
            send1((p, n), 2, blocks((p, n), 1, 1))
            send1((p, n), 3, blocks((p, n), -1, 0))
        multiply(n, [(0, 0)])
    x_cols.wait()
    for p in range(2):
        forward1((p, NQ - 1))
    for n in range(NQ - 1):
        for p in range(2):
            finish1((p, n))
        for p in range(2):
            forward2((p, n))
    for p in range(2):
        finish1((p, NQ - 1))
    for n in range(NQ - 1):
        for p in range(2):
            finish2((p, n))

    for cp in small_loads:
        cp.wait()
    r_dev = owners_ref.shape[1]
    eye = lax.broadcasted_iota(jnp.int32, (r_dev, r_dev), 0)
    eye_col = lax.broadcasted_iota(jnp.int32, (r_dev, r_dev), 1)
    same_place = eye == eye_col
    pick = jnp.sum(
        jnp.where(same_place, jnp.broadcast_to(picked_ref[...], (r_dev, r_dev)), 0), axis=1, keepdims=True
    )
    turns = jnp.broadcast_to(turn_ref[...], (r_dev, tokens))
    places = lax.broadcasted_iota(jnp.int32, (r_dev, tokens), 1)
    own_turn = jnp.sum(jnp.where(places == pick, turns, 0), axis=1, keepdims=True)
    member = jnp.where((turns == own_turn) & (places <= pick), 1.0, 0.0)
    count = jnp.sum(member, axis=1, keepdims=True)
    own_row = owners_ref[...]
    own_col = jnp.sum(
        jnp.where(same_place, jnp.broadcast_to(own_row, (r_dev, r_dev)), 0), axis=1, keepdims=True
    )
    rank = jnp.sum(jnp.where((own_col == own_row) & (eye < eye_col), 1, 0), axis=0, keepdims=True)
    cap = outb.shape[1]
    slot = own_row * cap + rank
    dispatch = jnp.where(
        lax.broadcasted_iota(jnp.int32, (n_head * cap, r_dev), 0) == slot, 1.0, 0.0
    ).astype(BF)

    for p in range(2):
        forward2((p, NQ - 1))
    for p in range(2):
        finish2((p, NQ - 1))

    summary = (mm(member.astype(BF), mixed_ref[...]) / count).astype(BF)
    outb[...] = mm(dispatch, summary).astype(BF).reshape(n_head, cap, col)
    mine = pl.ds(pl.multiple_of(me * col, col), col)
    keep = pltpu.make_async_copy(outb.at[me], inb.at[:, mine], msem.at[2])
    keep.start()

    def hand(i):
        to = lax.rem(me + i, n_head)
        return remote(outb.at[to], inb.at[:, mine], aas.at[i - 1], aar.at[i - 1], {"head": to})

    def hand_out(i, carry):
        hand(i).start()
        return carry

    lax.fori_loop(1, n_head, hand_out, 0)
    cand_load.wait()
    keep.wait()

    def take_in(i, carry):
        hand(i).wait()
        return carry

    lax.fori_loop(1, n_head, take_in, 0)
    scores_ref[...] = mm(inb[...], cand[...], ((1,), (1,)))

    for d in range(1, n_seq):

        @pl.when(z + d < n_seq)
        def _():
            for h in range(2):
                state_copy(d, h).wait_send()

    for cp in w2_remote + a2_copies + sends:
        cp.wait_send()


def hand_over(mixed_in, scores_in, mixed_out, scores_out, sem):
    copies = [
        pltpu.make_async_copy(mixed_in, mixed_out, sem.at[0]),
        pltpu.make_async_copy(scores_in, scores_out, sem.at[1]),
    ]
    for cp in copies:
        cp.start()
    for cp in copies:
        cp.wait()


def per_device(inputs, w_qkv, w_out, turn_ids, picked, owners, candidates):
    tokens, width = inputs.shape
    n_head = lax.axis_size("head")
    n_seq = lax.axis_size("seq")
    col = width // n_head
    here = w_qkv.shape[2]
    r_dev = picked.shape[1]
    cap = 4 * r_dev // n_head
    nk = width // KB
    units = 2 * NQ
    hp = tokens // (4 * NQ)
    dma = pltpu.SemaphoreType.DMA
    hbm = pl.BlockSpec(memory_space=pltpu.HBM)
    vmem = pl.BlockSpec(memory_space=pltpu.VMEM)
    results = pl.pallas_call(
        kernel,
        out_shape=(
            jax.ShapeDtypeStruct((tokens, col), BF),
            jax.ShapeDtypeStruct((cap, candidates.shape[0]), F32),
        ),
        in_specs=[hbm] * 7,
        out_specs=(vmem, vmem),
        scratch_shapes=[
            pltpu.VMEM((nk, tokens, KB), BF),
            pltpu.VMEM((nk, 3, KB, here), BF),
            pltpu.VMEM((3, tokens, here), F32),
            pltpu.VMEM((3, tokens, here), BF),
            pltpu.VMEM((2, HDIM, HDIM), BF),
            pltpu.VMEM((n_seq - 1, 2, HDIM, HDIM), BF),
            pltpu.VMEM((2, HDIM, HDIM), F32),
            pltpu.VMEM((tokens, here), F32),
            pltpu.VMEM((2, tokens, here), BF),
            pltpu.VMEM((SIDE, SIDE, 2, here, col), BF),
            pltpu.VMEM((SIDE, SIDE, tokens, col), BF),
            pltpu.VMEM((units, 6, SIDE, hp, col), BF),
            pltpu.VMEM((units, SIDE, 2 * hp, col), BF),
            pltpu.VMEM((units, 6, hp, col), BF),
            pltpu.VMEM((tokens, col), BF),
            pltpu.VMEM((n_head, cap, col), BF),
            pltpu.VMEM((cap, width), BF),
            pltpu.VMEM(candidates.shape, BF),
            pltpu.VMEM(turn_ids.shape, jnp.int32),
            pltpu.VMEM(picked.shape, jnp.int32),
            pltpu.VMEM((1, r_dev), jnp.int32),
            dma((nk,)),
            dma((nk,)),
            dma((nk,)),
            dma((6,)),
            dma((SIDE * SIDE,)),
            dma((SIDE * SIDE,)),
            dma((SIDE * SIDE,)),
            dma((2 * n_seq - 2,)),
            dma((2 * n_seq - 2,)),
            dma((NQ,)),
            dma((NQ,)),
            dma((units, 6)),
            dma((units, 6)),
            dma((units, 6)),
            dma((units, 6)),
            dma((n_head - 1,)),
            dma((n_head - 1,)),
        ],
        compiler_params=pltpu.CompilerParams(
            collective_id=0, has_side_effects=True, vmem_limit_bytes=53 << 20
        ),
    )(
        inputs,
        w_qkv,
        w_out,
        pltpu.with_memory_space_constraint(turn_ids, pltpu.HBM),
        pltpu.with_memory_space_constraint(picked, pltpu.HBM),
        pltpu.with_memory_space_constraint(owners.reshape(1, r_dev), pltpu.HBM),
        candidates,
    )
    return pl.pallas_call(
        hand_over,
        out_shape=tuple(jax.ShapeDtypeStruct(a.shape, a.dtype) for a in results),
        in_specs=[pl.BlockSpec(memory_space=pltpu.VMEM)] * 2,
        out_specs=(pl.BlockSpec(memory_space=pltpu.HBM),) * 2,
        scratch_shapes=[dma((2,))],
        compiler_params=pltpu.CompilerParams(vmem_limit_bytes=4 << 20),
    )(*results)


def solution(mesh):
    return jax.shard_map(
        per_device,
        mesh=mesh,
        in_specs=(
            P("seq", None),
            P(None, None, "head"),
            P("head", None),
            P("seq", None),
            P("seq", None),
            P("seq", None),
            P(("seq", "head"), None),
        ),
        out_specs=(P("seq", "head"), P(("seq", "head"), None)),
        check_vma=False,
    )
```

```python
import functools

import jax
import jax.numpy as jnp
from jax import lax
from jax.experimental import pallas as pl
from jax.experimental.pallas import tpu as pltpu
from jax.sharding import PartitionSpec as P

HDIM = 128
SIDE = 4
KB = 2048
AHEAD = 4
MEET = 3
NQ = 2
MESH = pl.DeviceIdType.MESH
BF = jnp.bfloat16
F32 = jnp.float32


def mm(a, b, dims=((1,), (0,))):
    return lax.dot_general(a, b, (dims, ((), ())), preferred_element_type=F32)


def kernel(
    x_hbm, wqkv_hbm, wout_hbm, turn_hbm, picked_hbm, owners_hbm, cand_hbm,
    mixed_ref, scores_ref,
    xbuf, wbuf, acc, qkv, st, st_in, carried, pre, a2, w2, c, r1, s1, r2, xcols, outb, inb, cand, turn_ref, picked_ref, owners_ref,
    xsem, wsem, qsem, msem, w2l, w2s, w2r, sts, strr, a2s, a2r, s1s, s1r, s2s, s2r, aas, aar,
):
    tokens, col = xcols.shape
    nk = xbuf.shape[0]
    n_head = outb.shape[0]
    n_seq = st_in.shape[0] + 1
    block = tokens // NQ
    piece = block // 2
    hp = piece // 2
    z = lax.axis_index("seq")
    me = lax.axis_index("head")
    core = lax.rem(me, 2)
    cy = lax.rem(lax.div(me, 2), SIDE)
    cx = lax.div(me, 2 * SIDE)

    def at(px, py, pc):
        return (px * SIDE + py) * 2 + pc

    sib = at(cx, cy, 1 - core)

    def x_load(k):
        return pltpu.make_async_copy(
            x_hbm.at[:, pl.ds(pl.multiple_of(k * KB, KB), KB)], xbuf.at[k], xsem.at[k]
        )

    def kv_load(k):
        rows = pl.ds(pl.multiple_of(k * KB, KB), KB)
        return pltpu.make_async_copy(
            wqkv_hbm.at[pl.ds(1, 2), rows, :], wbuf.at[k, pl.ds(1, 2)], wsem.at[k]
        )

    def q_load(k):
        rows = pl.ds(pl.multiple_of(k * KB, KB), KB)
        return pltpu.make_async_copy(wqkv_hbm.at[0, rows, :], wbuf.at[k, 0], qsem.at[k])

    def remote(src, dst, ssem, rsem, to):
        return pltpu.make_async_remote_copy(
            src_ref=src, dst_ref=dst, send_sem=ssem, recv_sem=rsem, device_id=to, device_id_type=MESH
        )

    for k in range(AHEAD):
        kv_load(k).start()
        x_load(k).start()

    barrier = pltpu.get_barrier_semaphore()

    def greet(i, carry):
        pl.semaphore_signal(
            barrier, inc=1, device_id={"head": lax.rem(me + i, n_head)}, device_id_type=MESH
        )
        return carry

    lax.fori_loop(1, n_head, greet, 0)
    for d in range(1, n_seq):
        pl.semaphore_signal(
            barrier, inc=1, device_id={"seq": lax.rem(z + d, n_seq)}, device_id_type=MESH
        )

    acc[...] = jnp.zeros_like(acc)

    def kv_step(k, carry):
        x_load(k).wait()
        kv_load(k).wait()

        @pl.when(k + AHEAD < nk)
        def _():
            kv_load(k + AHEAD).start()
            x_load(k + AHEAD).start()

        @pl.when(k + AHEAD >= nk)
        def _():
            q_load(k + AHEAD - nk).start()

        acc[1] += mm(xbuf[k], wbuf[k, 1])
        acc[2] += mm(xbuf[k], wbuf[k, 2])
        return carry

    lax.fori_loop(0, MEET, kv_step, 0)

    pl.semaphore_wait(barrier, n_head - 1 + n_seq - 1)

    w2_local, w2_remote = [], []
    for j in range(SIDE * SIDE):
        jx, jy = j // SIDE, j % SIDE
        mine = pl.ds(pl.multiple_of((2 * j + core) * col, col), col)
        theirs = pl.ds(pl.multiple_of((2 * j + 1 - core) * col, col), col)
        w2_local.append(
            pltpu.make_async_copy(wout_hbm.at[:, mine], w2.at[jx, jy, core], w2l.at[j])
        )
        w2_remote.append(
            remote(wout_hbm.at[:, theirs], w2.at[jx, jy, core], w2s.at[j], w2r.at[j], {"head": sib})
        )
    for cp in w2_local + w2_remote:
        cp.start()

    lax.fori_loop(MEET, nk, kv_step, 0)
    qkv[1] = acc[1].astype(BF)
    qkv[2] = acc[2].astype(BF)

    def state_copy(d, h):
        i = 2 * (d - 1) + h
        to = {"seq": lax.rem(z + d, n_seq)}
        return remote(st.at[h], st_in.at[d - 1, h], sts.at[i], strr.at[i], to)

    for h in range(2):
        hs = slice(h * HDIM, (h + 1) * HDIM)
        st[h] = mm(qkv[1, :, hs], qkv[2, :, hs], ((0,), (0,))).astype(BF)
        for d in range(1, n_seq):

            @pl.when(z + d < n_seq)
            def _():
                state_copy(d, h).start()

    x_cols = pltpu.make_async_copy(
        x_hbm.at[:, pl.ds(pl.multiple_of(me * col, col), col)], xcols, msem.at[0]
    )
    x_cols.start()
    cand_load = pltpu.make_async_copy(cand_hbm, cand, msem.at[1])
    cand_load.start()
    small_loads = [
        pltpu.make_async_copy(src, dst, msem.at[3 + i])
        for i, (src, dst) in enumerate(
            ((turn_hbm, turn_ref), (picked_hbm, picked_ref), (owners_hbm, owners_ref))
        )
    ]
    for cp in small_loads:
        cp.start()

    def q_step(k, carry):
        q_load(k).wait()

        @pl.when(k + AHEAD < nk)
        def _():
            q_load(k + AHEAD).start()

        acc[0] += mm(xbuf[k], wbuf[k, 0])
        return carry

    lax.fori_loop(0, nk, q_step, 0)
    qkv[0] = acc[0].astype(BF)

    def local(b):
        rows = slice(b * block, (b + 1) * block)
        seen = (b + 1) * block
        ok = (
            lax.broadcasted_iota(jnp.int32, (block, seen), 0) + b * block
            >= lax.broadcasted_iota(jnp.int32, (block, seen), 1)
        )
        for h in range(2):
            hs = slice(h * HDIM, (h + 1) * HDIM)
            sc = mm(qkv[0, rows, hs], qkv[1, :seen, hs], ((1,), (1,)))
            sc = jnp.where(ok, sc, 0.0).astype(BF)
            pre[rows, hs] = mm(sc, qkv[2, :seen, hs])

    def attend(b, prefix):
        rows = slice(b * block, (b + 1) * block)
        for h in range(2):
            hs = slice(h * HDIM, (h + 1) * HDIM)
            summed = pre[rows, hs] + mm(qkv[0, rows, hs], prefix[h])
            normed = summed * lax.rsqrt(jnp.mean(summed * summed, axis=-1, keepdims=True) + 1e-05)
            a2[core, rows, hs] = normed.astype(BF)
        cp = remote(a2.at[core, rows], a2.at[core, rows], a2s.at[b], a2r.at[b], {"head": sib})
        cp.start()
        return cp

    local(0)
    carried[...] = jnp.zeros_like(carried)
    for d in range(1, n_seq):

        @pl.when(z >= d)
        def _():
            for h in range(2):
                state_copy(d, h).wait_recv()
                carried[h] += st_in[d - 1, h].astype(F32)

    prefix = [carried[h].astype(BF) for h in range(2)]
    a2_copies = [attend(0, prefix)]
    for b in range(1, NQ):
        local(b)
        a2_copies.append(attend(b, prefix))
    for cp in w2_local:
        cp.wait()
    for cp in w2_remote:
        cp.wait_recv()

    spot = (cx, cy)

    def turn(p, by):
        return lax.rem(spot[p] + by + SIDE, SIDE)

    def neighbour(p, by):
        to = turn(p, by)
        return {"head": at(to, cy, core) if p == 0 else at(cx, to, core)}

    def multiply(n, places):
        rows = slice(n * block, (n + 1) * block)
        left = jnp.concatenate([a2[0, rows], a2[1, rows]], axis=1)
        for bx, by in places:
            jx, jy = turn(0, bx), turn(1, by)
            right = w2[jx, jy].reshape(left.shape[1], col)
            c[jx, jy, rows, :] = mm(left, right).astype(BF)

    pieces = [(p, n) for n in range(NQ) for p in range(2)]
    index = {u: i for i, u in enumerate(pieces)}
    sends = []

    def part(u, which):
        p, n = u
        start = n * block + p * piece + which * hp
        return slice(start, start + hp)

    def blocks(u, by, which):
        i = turn(u[0], by)
        rows = part(u, which)
        return c.at[i, :, rows, :] if u[0] == 0 else c.at[:, i, rows, :]

    def send1(u, kind, src):
        i = index[u]
        cp = remote(
            src, r1.at[i, kind], s1s.at[i, kind], s1r.at[i, kind], neighbour(u[0], (1, -1)[kind % 2])
        )
        cp.start()
        sends.append(cp)

    def got1(u, kind):
        i = index[u]
        remote(
            r1.at[i, kind], r1.at[i, kind], s1s.at[i, kind], s1r.at[i, kind], neighbour(u[0], 1)
        ).wait_recv()

    def send2(u, kind, src):
        i = index[u]
        cp = remote(
            src, r2.at[i, kind], s2s.at[i, kind], s2r.at[i, kind], neighbour(1 - u[0], (1, -1)[kind % 2])
        )
        cp.start()
        sends.append(cp)

    def got2(u, kind):
        i = index[u]
        remote(
            r2.at[i, kind], r2.at[i, kind], s2s.at[i, kind], s2r.at[i, kind], neighbour(1 - u[0], 1)
        ).wait_recv()

    def forward1(u):
        i = index[u]
        for kind, by, which in ((0, 1, 0), (1, -1, 1)):
            got1(u, kind)
            r1[i, kind] = (
                r1[i, kind].astype(F32) + blocks(u, by, which)[...].astype(F32)
            ).astype(BF)
            send1(u, kind + 4, r1.at[i, kind])

    def finish1(u):
        i = index[u]
        for kind in (2, 3, 4, 5):
            got1(u, kind)
        for which, one, two in ((0, 4, 3), (1, 5, 2)):
            s1[i, :, which * hp : (which + 1) * hp, :] = (
                blocks(u, 0, which)[...].astype(F32) + r1[i, one].astype(F32) + r1[i, two].astype(F32)
            ).astype(BF)
        rows = (slice(0, hp), slice(hp, 2 * hp))
        q = 1 - u[0]
        send2(u, 0, s1.at[i, turn(q, 2), rows[0]])
        send2(u, 1, s1.at[i, turn(q, 2), rows[1]])
        send2(u, 2, s1.at[i, turn(q, 1), rows[1]])
        send2(u, 3, s1.at[i, turn(q, -1), rows[0]])

    def forward2(u):
        i = index[u]
        q = 1 - u[0]
        for kind, by, rows in ((0, 1, slice(0, hp)), (1, -1, slice(hp, 2 * hp))):
            got2(u, kind)
            r2[i, kind] = (
                r2[i, kind].astype(F32) + s1[i, turn(q, by), rows].astype(F32)
            ).astype(BF)
            send2(u, kind + 4, r2.at[i, kind])

    def finish2(u):
        i = index[u]
        for kind in (2, 3, 4, 5):
            got2(u, kind)
        q = 1 - u[0]
        for which, one, two in ((0, 4, 3), (1, 5, 2)):
            rows = part(u, which)
            branch = (
                s1[i, turn(q, 0), which * hp : (which + 1) * hp].astype(F32)
                + r2[i, one].astype(F32)
                + r2[i, two].astype(F32)
            )
            mixed_ref[rows, :] = (xcols[rows, :].astype(F32) + branch).astype(BF)

    steps = (2, 1, -1, 0)
    first = [(2, b) for b in steps] + [(b, 2) for b in steps[1:]]
    second = [(a, b) for a in steps[1:] for b in steps[1:] if (a, b) != (0, 0)]

    for n in range(NQ):
        a2_copies[n].wait_recv()
        multiply(n, first)
        for p in range(2):
            send1((p, n), 0, blocks((p, n), 2, 0))
            send1((p, n), 1, blocks((p, n), 2, 1))
        if n > 0:
            for p in range(2):
                forward1((p, n - 1))
        multiply(n, second)
        for p in range(2):
            send1((p, n), 2, blocks((p, n), 1, 1))
            send1((p, n), 3, blocks((p, n), -1, 0))
        multiply(n, [(0, 0)])
    x_cols.wait()
    for p in range(2):
        forward1((p, NQ - 1))
    for n in range(NQ - 1):
        for p in range(2):
            finish1((p, n))
        for p in range(2):
            forward2((p, n))
    for p in range(2):
        finish1((p, NQ - 1))
    for n in range(NQ - 1):
        for p in range(2):
            finish2((p, n))

    for cp in small_loads:
        cp.wait()
    r_dev = owners_ref.shape[1]
    eye = lax.broadcasted_iota(jnp.int32, (r_dev, r_dev), 0)
    eye_col = lax.broadcasted_iota(jnp.int32, (r_dev, r_dev), 1)
    same_place = eye == eye_col
    pick = jnp.sum(
        jnp.where(same_place, jnp.broadcast_to(picked_ref[...], (r_dev, r_dev)), 0), axis=1, keepdims=True
    )
    turns = jnp.broadcast_to(turn_ref[...], (r_dev, tokens))
    places = lax.broadcasted_iota(jnp.int32, (r_dev, tokens), 1)
    own_turn = jnp.sum(jnp.where(places == pick, turns, 0), axis=1, keepdims=True)
    member = jnp.where((turns == own_turn) & (places <= pick), 1.0, 0.0)
    count = jnp.sum(member, axis=1, keepdims=True)
    own_row = owners_ref[...]
    own_col = jnp.sum(
        jnp.where(same_place, jnp.broadcast_to(own_row, (r_dev, r_dev)), 0), axis=1, keepdims=True
    )
    rank = jnp.sum(jnp.where((own_col == own_row) & (eye < eye_col), 1, 0), axis=0, keepdims=True)
    cap = outb.shape[1]
    slot = own_row * cap + rank
    dispatch = jnp.where(
        lax.broadcasted_iota(jnp.int32, (n_head * cap, r_dev), 0) == slot, 1.0, 0.0
    ).astype(BF)

    for p in range(2):
        forward2((p, NQ - 1))
    for p in range(2):
        finish2((p, NQ - 1))

    summary = (mm(member.astype(BF), mixed_ref[...]) / count).astype(BF)
    outb[...] = mm(dispatch, summary).astype(BF).reshape(n_head, cap, col)
    mine = pl.ds(pl.multiple_of(me * col, col), col)
    keep = pltpu.make_async_copy(outb.at[me], inb.at[:, mine], msem.at[2])
    keep.start()

    def hand(i):
        to = lax.rem(me + i, n_head)
        return remote(outb.at[to], inb.at[:, mine], aas.at[i - 1], aar.at[i - 1], {"head": to})

    def hand_out(i, carry):
        hand(i).start()
        return carry

    lax.fori_loop(1, n_head, hand_out, 0)
    cand_load.wait()
    keep.wait()

    def take_in(i, carry):
        hand(i).wait()
        return carry

    lax.fori_loop(1, n_head, take_in, 0)
    scores_ref[...] = mm(inb[...], cand[...], ((1,), (1,)))

    for d in range(1, n_seq):

        @pl.when(z + d < n_seq)
        def _():
            for h in range(2):
                state_copy(d, h).wait_send()

    for cp in w2_remote + a2_copies + sends:
        cp.wait_send()


def hand_over(mixed_in, scores_in, mixed_out, scores_out, sem):
    copies = [
        pltpu.make_async_copy(mixed_in, mixed_out, sem.at[0]),
        pltpu.make_async_copy(scores_in, scores_out, sem.at[1]),
    ]
    for cp in copies:
        cp.start()
    for cp in copies:
        cp.wait()


def per_device(inputs, w_qkv, w_out, turn_ids, picked, owners, candidates):
    tokens, width = inputs.shape
    n_head = lax.axis_size("head")
    n_seq = lax.axis_size("seq")
    col = width // n_head
    here = w_qkv.shape[2]
    r_dev = picked.shape[1]
    cap = 4 * r_dev // n_head
    nk = width // KB
    units = 2 * NQ
    hp = tokens // (4 * NQ)
    dma = pltpu.SemaphoreType.DMA
    hbm = pl.BlockSpec(memory_space=pltpu.HBM)
    vmem = pl.BlockSpec(memory_space=pltpu.VMEM)
    results = pl.pallas_call(
        kernel,
        out_shape=(
            jax.ShapeDtypeStruct((tokens, col), BF),
            jax.ShapeDtypeStruct((cap, candidates.shape[0]), F32),
        ),
        in_specs=[hbm] * 7,
        out_specs=(vmem, vmem),
        scratch_shapes=[
            pltpu.VMEM((nk, tokens, KB), BF),
            pltpu.VMEM((nk, 3, KB, here), BF),
            pltpu.VMEM((3, tokens, here), F32),
            pltpu.VMEM((3, tokens, here), BF),
            pltpu.VMEM((2, HDIM, HDIM), BF),
            pltpu.VMEM((n_seq - 1, 2, HDIM, HDIM), BF),
            pltpu.VMEM((2, HDIM, HDIM), F32),
            pltpu.VMEM((tokens, here), F32),
            pltpu.VMEM((2, tokens, here), BF),
            pltpu.VMEM((SIDE, SIDE, 2, here, col), BF),
            pltpu.VMEM((SIDE, SIDE, tokens, col), BF),
            pltpu.VMEM((units, 6, SIDE, hp, col), BF),
            pltpu.VMEM((units, SIDE, 2 * hp, col), BF),
            pltpu.VMEM((units, 6, hp, col), BF),
            pltpu.VMEM((tokens, col), BF),
            pltpu.VMEM((n_head, cap, col), BF),
            pltpu.VMEM((cap, width), BF),
            pltpu.VMEM(candidates.shape, BF),
            pltpu.VMEM(turn_ids.shape, jnp.int32),
            pltpu.VMEM(picked.shape, jnp.int32),
            pltpu.VMEM((1, r_dev), jnp.int32),
            dma((nk,)),
            dma((nk,)),
            dma((nk,)),
            dma((6,)),
            dma((SIDE * SIDE,)),
            dma((SIDE * SIDE,)),
            dma((SIDE * SIDE,)),
            dma((2 * n_seq - 2,)),
            dma((2 * n_seq - 2,)),
            dma((NQ,)),
            dma((NQ,)),
            dma((units, 6)),
            dma((units, 6)),
            dma((units, 6)),
            dma((units, 6)),
            dma((n_head - 1,)),
            dma((n_head - 1,)),
        ],
        compiler_params=pltpu.CompilerParams(
            collective_id=0, has_side_effects=True, vmem_limit_bytes=53 << 20
        ),
    )(
        inputs,
        w_qkv,
        w_out,
        pltpu.with_memory_space_constraint(turn_ids, pltpu.HBM),
        pltpu.with_memory_space_constraint(picked, pltpu.HBM),
        pltpu.with_memory_space_constraint(owners.reshape(1, r_dev), pltpu.HBM),
        candidates,
    )
    return pl.pallas_call(
        hand_over,
        out_shape=tuple(jax.ShapeDtypeStruct(a.shape, a.dtype) for a in results),
        in_specs=[pl.BlockSpec(memory_space=pltpu.VMEM)] * 2,
        out_specs=(pl.BlockSpec(memory_space=pltpu.HBM),) * 2,
        scratch_shapes=[dma((2,))],
        compiler_params=pltpu.CompilerParams(vmem_limit_bytes=4 << 20),
    )(*results)


def solution(mesh):
    return jax.shard_map(
        per_device,
        mesh=mesh,
        in_specs=(
            P("seq", None),
            P(None, None, "head"),
            P("head", None),
            P("seq", None),
            P("seq", None),
            P("seq", None),
            P(("seq", "head"), None),
        ),
        out_specs=(P("seq", "head"), P(("seq", "head"), None)),
        check_vma=False,
    )
```
